128 devices in a mesh: group: 8 (over y, core), member: 16 (over z, x).
Axes of the slice: x: 4, y: 4, z: 4, core: 2. Of those that a mesh axis runs over, the one named last changes fastest.
Arguments:
- feats: bfloat16 [96, 524288], P(None, ('group', 'member')), may hold values from -6 to 6
- kmap: int32 [27, 524288], P(None, ('group', 'member')), may hold values from 0 to 5888, as said below
- send_rows: int32 [128, 7, 256], P(('group', 'member')), may hold values from 0 to 4095
- w_sub: bfloat16 [27, 96, 96], replicated, may hold values from -0.125 to 0.125
- owner: int32 [524288, 1], P(('group', 'member')), may hold values from 0 to 127, as said below
- coarse_id: int32 [524288], P(('group', 'member')), may hold values from 0 to 511
- octant: int32 [524288], P(('group', 'member')), may hold values from 0 to 7
- w_down: bfloat16 [8, 192, 96], replicated, may hold values from -0.21875 to 0.21875
- grad_coarse: bfloat16 [192, 65536], P(None, ('group', 'member')), may hold values from -6 to 6
Outputs:
- coarse_out: bfloat16 [192, 65536], P(None, ('group', 'member'))
- grad_feats: float32 [96, 524288], P(None, ('group', 'member'))
- grad_w_sub: float32 [27, 96, 96], replicated
- grad_w_down: float32 [8, 192, 96], replicated
The draws below stay inside these ranges and needn't reach their ends.
Inputs may be any that keep to these rules, and one draw needn't show every extreme that they name: kmap[k, v] indexes the table of v's device: below 4096 a voxel of that device, then 256 received voxels for each of the 7 levels in order, and 5888 for a missing neighbour; kmap[13, v] is v's own column. owner[v, 0] is v's own device or its partner at one of the 7 levels; among the voxels of one device at most 128 name its partner of any one level, and on every device some level's partner is named by exactly 128.
All inputs are finite; a program needn't handle non-finite values.
Results may differ from the reference program's by a relative error of at most 0.0056.
Values may be sent and summed in bfloat16 or wider, within the bound.
No kernel may reach another device: no remote copies, remote signals or barrier semaphores. Data moves between devices by JAX's collectives and lax.ppermute only.
A program may use at most 128 MiB of HBM per device.

```python
import jax
import jax.numpy as jnp
from jax import lax

C1 = 96
C2 = 192
KVOL = 27
OCT = 8
V_DEV = 4096
LEVELS = 7
HALO_CAP = 256
COARSE_DEV = 512
CAP2 = 128
V_TOTAL = 524288
COARSE = 65536
DEVICES = 128


def draw_kmap(key, part):
    key_pick, key_local, key_halo = jax.random.split(key, 3)
    shape = (KVOL, V_TOTAL)
    pick = jax.random.randint(key_pick, shape, 0, 100)
    local = jax.random.randint(key_local, shape, 0, V_DEV)
    remote = jax.random.randint(key_halo, shape, V_DEV, V_DEV + LEVELS * HALO_CAP)
    empty = jnp.full(shape, V_DEV + LEVELS * HALO_CAP, jnp.int32)
    table = jnp.where(pick < 55, local, jnp.where(pick < 80, remote, empty))
    itself = (jnp.arange(V_TOTAL, dtype=jnp.int32) % V_DEV)[None, :]
    center = (jnp.arange(KVOL, dtype=jnp.int32) == KVOL // 2)[:, None]
    return jnp.where(center, itself, table).astype(jnp.int32)


def draw_owner(key, part):
    key_count, key_full, key_perm = jax.random.split(jax.random.fold_in(key, 17), 3)
    counts = jax.random.randint(key_count, (DEVICES, LEVELS), CAP2 // 4, CAP2 + 1)
    full_level = jax.random.randint(key_full, (DEVICES,), 0, LEVELS)
    level_ids = jnp.arange(LEVELS, dtype=jnp.int32)
    counts = jnp.where(level_ids[None, :] == full_level[:, None], CAP2, counts).astype(jnp.int32)
    ends = jnp.cumsum(counts, axis=1).astype(jnp.int32)
    perm_keys = jax.random.split(key_perm, DEVICES)
    shuffled = jax.vmap(lambda k: jax.random.permutation(k, V_DEV))(perm_keys).astype(jnp.int32)
    ranking = jnp.argsort(shuffled, axis=1, stable=True).astype(jnp.int32)
    level = jnp.sum((ranking[:, :, None] >= ends[:, None, :]).astype(jnp.int32), axis=2)
    device = jnp.arange(DEVICES, dtype=jnp.int32)[:, None]
    partner = jnp.bitwise_xor(device, jnp.left_shift(jnp.int32(1), jnp.minimum(level, LEVELS - 1)))
    result = jnp.where(level < LEVELS, partner, device)
    return result.reshape(V_TOTAL, 1).astype(jnp.int32)


def set_ends(entries, rng, least, largest):
    place = [jax.random.randint(jax.random.fold_in(rng, axis), (), 0, length) for axis, length in enumerate(entries.shape)]
    widest = entries.shape.index(max(entries.shape))
    next_to = place[:widest] + [(place[widest] + 1) % entries.shape[widest]] + place[widest + 1:]
    return entries.at[tuple(place)].set(least).at[tuple(next_to)].set(largest)


def block_scale(stream_key, extent, cuts, low, top_value):
    def one(dim, blocks):
        draws = jax.random.uniform(jax.random.fold_in(jax.random.fold_in(stream_key, 6), dim), (blocks,), jnp.float32, low / len(cuts), top_value / len(cuts))
        return jnp.repeat(jnp.exp(draws), extent[dim] // blocks).reshape((-1,) + (1,) * (len(extent) - dim - 1))

    loudness = one(*cuts[0])
    for cut in cuts[1:]:
        loudness = loudness * one(*cut)
    return loudness


def bell_draw(own_key, extent, deviation, most, cuts=(), kind=jnp.bfloat16):
    loudness = block_scale(own_key, extent, cuts, -0.22, 0.18) if cuts else 1.0
    drawn = jax.random.normal(own_key, extent, jnp.float32) * deviation * loudness
    return jnp.minimum(jnp.maximum(drawn, -most), most).astype(kind)


def setup_inputs(seed: int = 0) -> dict:
    streams_of = jax.random.split(jax.random.key(seed), 10)
    return {
        "feats": bell_draw(streams_of[0], (C1, V_TOTAL), 1.0, 6.0, ((1, 128),)),
        "kmap": draw_kmap(jax.random.fold_in(streams_of[9], 71), 0),
        "send_rows": set_ends(jax.random.randint(streams_of[2], (DEVICES, LEVELS, HALO_CAP), 0, V_DEV), jax.random.fold_in(streams_of[2], 1), 0, V_DEV - 1).astype(jnp.int32),
        "w_sub": bell_draw(streams_of[3], (KVOL, C1, C1), (KVOL * C1) ** -0.5, 0.125),
        "owner": draw_owner(jax.random.fold_in(streams_of[9], 71), 0),
        "coarse_id": set_ends(jax.random.randint(streams_of[5], (V_TOTAL,), 0, COARSE_DEV), jax.random.fold_in(streams_of[5], 1), 0, COARSE_DEV - 1).astype(jnp.int32),
        "octant": set_ends(jax.random.randint(streams_of[6], (V_TOTAL,), 0, OCT), jax.random.fold_in(streams_of[6], 1), 0, OCT - 1).astype(jnp.int32),
        "w_down": bell_draw(streams_of[7], (OCT, C2, C1), (OCT * C1) ** -0.5, 0.21875),
        "grad_coarse": bell_draw(streams_of[8], (C2, COARSE), 1.0, 6.0, ((1, 128),)),
    }


def neighbour_ids(kmap, send_rows):
    columns = jnp.arange(V_TOTAL, dtype=jnp.int32)
    device = (columns // V_DEV)[None, :]
    limit = V_DEV + LEVELS * HALO_CAP
    spot = jnp.clip(kmap - V_DEV, 0, LEVELS * HALO_CAP - 1)
    level = spot // HALO_CAP
    slot = spot % HALO_CAP
    partner = jnp.bitwise_xor(device, jnp.left_shift(jnp.int32(1), level))
    remote = partner * V_DEV + send_rows[partner, level, slot]
    local = device * V_DEV + kmap
    empty = jnp.full(kmap.shape, V_TOTAL, jnp.int32)
    return jnp.where(kmap < V_DEV, local, jnp.where(kmap < limit, remote, empty)).astype(jnp.int32)


def reference(feats, kmap, send_rows, w_sub, owner, coarse_id, octant, w_down, grad_coarse):
    src = neighbour_ids(kmap, send_rows)
    padded = jnp.concatenate([feats, jnp.zeros((C1, 1), jnp.bfloat16)], axis=1)

    def forward_step(total, inputs):
        weight, cols = inputs
        taken = jnp.take(padded, cols, axis=1)
        return total + jnp.dot(weight, taken, preferred_element_type=jnp.float32), None

    pre, _ = lax.scan(forward_step, jnp.zeros((C1, V_TOTAL), jnp.float32), (w_sub, src))
    y1 = jax.nn.silu(pre).astype(jnp.bfloat16)
    keys = (octant * COARSE + owner[:, 0] * COARSE_DEV + coarse_id).astype(jnp.int32)
    pooled = jnp.zeros((C1, OCT * COARSE), jnp.float32).at[:, keys].add(y1.astype(jnp.float32))
    pooled = pooled.astype(jnp.bfloat16).reshape(C1, OCT, COARSE)
    coarse_out = jnp.einsum("oci,ion->cn", w_down.astype(jnp.float32), pooled.astype(jnp.float32)).astype(jnp.bfloat16)
    grad_w_down = jnp.einsum("cn,ion->oci", grad_coarse.astype(jnp.float32), pooled.astype(jnp.float32))
    grad_pooled = jnp.einsum("oci,cn->ion", w_down.astype(jnp.float32), grad_coarse.astype(jnp.float32))
    grad_pooled = grad_pooled.astype(jnp.bfloat16).reshape(C1, OCT * COARSE)
    grad_y1 = jnp.take(grad_pooled, keys, axis=1)
    sig = jax.nn.sigmoid(pre)
    grad_pre = (grad_y1.astype(jnp.float32) * (sig * (1.0 + pre * (1.0 - sig)))).astype(jnp.bfloat16)

    def backward_step(grad_all, inputs):
        weight, cols = inputs
        taken = jnp.take(padded, cols, axis=1)
        dweight = jnp.dot(grad_pre, taken.T, preferred_element_type=jnp.float32)
        contrib = jnp.dot(weight.T, grad_pre, preferred_element_type=jnp.float32)
        return grad_all.at[:, cols].add(contrib), dweight

    grad_all, grad_w_sub = lax.scan(backward_step, jnp.zeros((C1, V_TOTAL + 1), jnp.float32), (w_sub, src))
    return coarse_out, grad_all[:, :V_TOTAL], grad_w_sub, grad_w_down
```

```python
import functools

import jax
import jax.numpy as jnp
from jax import lax
from jax.experimental import pallas as pl
from jax.experimental.pallas import tpu as pltpu
from jax.sharding import PartitionSpec as P

LANES = 128
SUB = 8
DIGIT = 64
SMEM = pltpu.SMEM
F32 = jnp.float32
BF16 = jnp.bfloat16
I32 = jnp.int32


def from_partner(value, level, bits_member):
    axis, stride = ("member", level) if level < bits_member else ("group", level - bits_member)
    mask = 2**stride
    pairs = [(source, source ^ mask) for source in range(lax.axis_size(axis))]
    return lax.ppermute(value, axis, pairs)


def vmem_full(shape):
    return pl.BlockSpec(shape, lambda *_: (0,) * len(shape))


def smem_full(shape):
    return pl.BlockSpec(shape, lambda *_: (0,) * len(shape), memory_space=SMEM)


def copy_rows(count, unroll, index, source, target):
    def body(step, _):
        base = pl.multiple_of(step * unroll, unroll)
        for j in range(unroll):
            target[pl.ds(base + j, 1), :] = source[pl.ds(index(base + j), 1), :]
        return 0

    lax.fori_loop(0, count // unroll, body, 0)


def add_rows(count, unroll, index, source, tables):
    lanes = len(tables)

    def body(step, _):
        base = pl.multiple_of(step * unroll, unroll)
        for start in range(0, unroll, lanes):
            spots = [index(base + start + j) for j in range(lanes)]
            sums = [
                tables[j][pl.ds(spots[j], 1), :] + source[pl.ds(base + start + j, 1), :]
                for j in range(lanes)
            ]
            for j in range(lanes):
                tables[j][pl.ds(spots[j], 1), :] = sums[j]
        return 0

    lax.fori_loop(0, count // unroll, body, 0)


def prepare_kernel(levels, me_ref, rows_ref, owner_ref, coarse_ref, octant_ref, feats_ref, *refs, coarse_dev, slots):
    messages = refs[:levels]
    table_ref, pos_ref, parent_ref, self_ref, buf = refs[levels:]
    chans, vdev = feats_ref.shape
    halo = rows_ref.shape[1] // levels
    noct_keys = 8 * coarse_dev
    fill = jnp.zeros((LANES - chans, LANES), F32)
    for c in range(vdev // LANES):
        cols = pl.ds(c * LANES, LANES)
        block = jnp.concatenate([feats_ref[:, cols].astype(F32), fill], axis=0)
        table_ref[cols, :] = block.T
    copy_rows(levels * halo, 64, lambda r: rows_ref[0, r], table_ref, buf)

    differ = jnp.bitwise_xor(owner_ref[...], me_ref[0])
    level_id = lax.broadcasted_iota(I32, (SUB, LANES), 0)
    bit = jnp.where(level_id < levels, jnp.left_shift(jnp.ones_like(level_id), level_id), 0)
    chunks = vdev // LANES
    classes = []
    for c in range(chunks):
        part = jnp.broadcast_to(differ[:, c * LANES : (c + 1) * LANES], (SUB, LANES))
        classes.append(jnp.where((part == bit) & (level_id < levels), 1.0, 0.0).astype(F32))
    upper = lax.broadcasted_iota(I32, (LANES, LANES), 0) <= lax.broadcasted_iota(I32, (LANES, LANES), 1)
    prefix = jnp.dot(
        jnp.concatenate(classes, axis=0).astype(BF16),
        jnp.where(upper, 1.0, 0.0).astype(BF16),
        preferred_element_type=F32,
    )
    carry = jnp.zeros((SUB, 1), F32)
    start = (level_id * slots).astype(F32)
    digit_rows = []
    digit_id = lax.broadcasted_iota(I32, (SUB, LANES), 0)
    for c in range(chunks):
        cols = pl.ds(c * LANES, LANES)
        inclusive = prefix[c * SUB : (c + 1) * SUB]
        spot = classes[c] * (start + inclusive - 1.0 + carry)
        carry = carry + inclusive[:, LANES - 1 :]
        remote = jnp.sum(classes[c], axis=0, keepdims=True) > 0.5
        position = jnp.where(remote, jnp.sum(spot, axis=0, keepdims=True).astype(I32), levels * slots)
        keys = octant_ref[:, cols] * coarse_dev + coarse_ref[:, cols]
        pos_ref[:, cols] = position
        parent_ref[:, cols] = jnp.where(remote, noct_keys + position, keys)
        self_ref[:, cols] = jnp.where(remote, noct_keys, keys)
        high = jnp.broadcast_to(lax.shift_right_logical(keys, 6) - DIGIT, (SUB, LANES))
        low = jnp.broadcast_to(keys & (DIGIT - 1), (SUB, LANES))
        digits = jnp.where(digit_id == 0, high, jnp.where(digit_id == 1, low, 0))
        digit_rows.append(digits.astype(F32).astype(BF16))
    digits = jnp.concatenate(digit_rows, axis=1)
    slot_id = lax.broadcasted_iota(I32, (slots, LANES), 0)
    for level in range(levels):
        hot = []
        for c in range(chunks):
            position = jnp.broadcast_to(pos_ref[:, pl.ds(c * LANES, LANES)], (slots, LANES))
            hot.append(jnp.where(position == slot_id + level * slots, 1.0, 0.0).astype(BF16))
        found = lax.dot_general(
            digits, jnp.concatenate(hot, axis=1), (((1,), (1,)), ((), ())), preferred_element_type=F32
        )
        found = found + jnp.where(digit_id == 0, float(DIGIT), 0.0)
        messages[level][pl.ds(0, halo), :] = buf[pl.ds(level * halo, halo), :].astype(BF16)
        messages[level][pl.ds(halo, 2 * SUB), :] = jnp.concatenate(
            [found, jnp.zeros((SUB, LANES), F32)], axis=0
        ).astype(BF16)


def parents_kernel(levels, keys_ref, coarse_ref, weight_ref, *refs):
    outs = refs[:levels]
    table_ref, wide, buf = refs[levels:]
    noct = weight_ref.shape[0]
    ndev = coarse_ref.shape[0]
    slots = outs[0].shape[0]
    for o in range(noct):
        grad = jnp.dot(coarse_ref[...], weight_ref[o], preferred_element_type=F32)
        grad = grad.astype(BF16).astype(F32)
        table_ref[pl.ds(o * ndev, ndev), :] = grad
        wide[pl.ds(o * ndev, ndev), :] = grad
    wide[pl.ds(noct * ndev, SUB), :] = jnp.zeros((SUB, LANES), F32)
    copy_rows(levels * slots, 64, lambda r: keys_ref[0, r], wide, buf)
    for level in range(levels):
        outs[level][...] = buf[pl.ds(level * slots, slots), :].astype(BF16)


def gather_kernel(levels, halo, index_ref, local_ref, *refs):
    received = refs[:levels]
    out_ref, table, buf = refs[levels:]
    vdev = local_ref.shape[0]

    @pl.when(pl.program_id(0) == 0)
    def _():
        table[pl.ds(0, vdev), :] = local_ref[...]
        for level in range(levels):
            table[pl.ds(vdev + level * halo, halo), :] = received[level][pl.ds(0, halo), :].astype(F32)
        table[pl.ds(vdev + levels * halo, SUB), :] = jnp.zeros((SUB, LANES), F32)

    chunk = buf.shape[0]

    def body(step, _):
        base = pl.multiple_of(step * chunk, chunk)
        for j in range(chunk):
            buf[pl.ds(j, 1), :] = table[pl.ds(index_ref[0, 0, base + j], 1), :]
        out_ref[pl.ds(base, chunk), :] = buf[...].astype(BF16)
        return 0

    lax.fori_loop(0, vdev // chunk, body, 0)


def middle_kernel(levels, parent_ref, pos_ref, self_ref, pre_ref, table_ref, *refs, tables):
    returned = refs[:levels]
    grad_ref, pool_ref = refs[levels : levels + 2]
    sends = refs[levels + 2 : 2 * levels + 2]
    wide, rows, act, out = refs[2 * levels + 2 : 2 * levels + 6]
    pools = refs[2 * levels + 6 :]
    vdev = pre_ref.shape[0]
    keys = table_ref.shape[0]
    slots = returned[0].shape[0]
    wide[pl.ds(0, keys), :] = table_ref[...]
    for level in range(levels):
        wide[pl.ds(keys + level * slots, slots), :] = returned[level][...].astype(F32)
    copy_rows(vdev, 64, lambda r: parent_ref[0, r], wide, rows)

    def point(step, _):
        part = pl.ds(pl.multiple_of(step * 256, 256), 256)
        pre = pre_ref[part, :]
        sig = 1.0 / (1.0 + jnp.exp(-pre))
        act[part, :] = (pre * sig).astype(BF16).astype(F32)
        grad_ref[part, :] = (rows[part, :] * (sig * (1.0 + pre * (1.0 - sig)))).astype(BF16)
        return 0

    lax.fori_loop(0, vdev // 256, point, 0)

    def send(step, _):
        base = pl.multiple_of(step * 64, 64)
        for j in range(64):
            out[pl.ds(pos_ref[0, base + j], 1), :] = act[pl.ds(base + j, 1), :]
        return 0

    out[...] = jnp.zeros_like(out)
    lax.fori_loop(0, vdev // 64, send, 0)
    for level in range(levels):
        sends[level][...] = out[pl.ds(level * slots, slots), :].astype(BF16)
    for pool in pools:
        pool[...] = jnp.zeros_like(pool)
    add_rows(vdev, 64, lambda r: self_ref[0, r], act, pools)
    total = pools[0][pl.ds(0, keys), :]
    for pool in pools[1:]:
        total = total + pool[pl.ds(0, keys), :]
    pool_ref[...] = total


def pool_kernel(levels, keys_ref, pool_ref, grad_ref, weight_ref, *refs):
    received = refs[:levels]
    coarse_ref, down_ref, rows = refs[levels : levels + 3]
    pools = refs[levels + 3 :]
    slots = received[0].shape[0]
    noct, _, chans = down_ref.shape
    ndev = grad_ref.shape[1]
    for level in range(levels):
        rows[pl.ds(level * slots, slots), :] = received[level][...].astype(F32)
    for pool in pools:
        pool[...] = jnp.zeros_like(pool)
    add_rows(levels * slots, 64, lambda r: keys_ref[0, r], rows, pools)
    coarse = jnp.zeros(coarse_ref.shape, F32)
    for o in range(noct):
        part = pl.ds(o * ndev, ndev)
        total = pool_ref[part, :]
        for pool in pools:
            total = total + pool[part, :]
        pooled = total.astype(BF16)
        coarse = coarse + lax.dot_general(
            weight_ref[o], pooled, (((1,), (1,)), ((), ())), preferred_element_type=F32
        )
        down = jnp.dot(grad_ref[...], pooled, preferred_element_type=F32)
        down_ref[o] = down[:, :chans]
    coarse_ref[...] = coarse.astype(BF16)


def scatter_kernel(levels, halo, index_ref, terms_ref, local_ref, *refs):
    backs = refs[:levels]
    tables = refs[levels:]
    vdev = local_ref.shape[0]

    @pl.when(pl.program_id(0) == 0)
    def _():
        for table in tables:
            table[...] = jnp.zeros_like(table)

    add_rows(vdev, 64, lambda r: index_ref[0, 0, r], terms_ref, tables)

    @pl.when(pl.program_id(0) == pl.num_programs(0) - 1)
    def _():
        def total(part):
            result = tables[0][part, :]
            for table in tables[1:]:
                result = result + table[part, :]
            return result

        local_ref[...] = total(pl.ds(0, vdev))
        for level in range(levels):
            backs[level][...] = total(pl.ds(vdev + level * halo, halo)).astype(BF16)


def finish_kernel(levels, rows_ref, local_ref, *refs):
    incoming = refs[:levels]
    out_ref, rows = refs[levels : levels + 2]
    tables = refs[levels + 2 :]
    halo = incoming[0].shape[0]
    chans, vdev = out_ref.shape
    for level in range(levels):
        rows[pl.ds(level * halo, halo), :] = incoming[level][...].astype(F32)
    for table in tables:
        table[...] = jnp.zeros_like(table)
    add_rows(levels * halo, 64, lambda r: rows_ref[0, r], rows, tables)
    for c in range(vdev // LANES):
        part = pl.ds(c * LANES, LANES)
        total = local_ref[part, :]
        for table in tables:
            total = total + table[part, :]
        out_ref[:, part] = total.T[:chans]


def shape(dims, dtype):
    return jax.ShapeDtypeStruct(dims, dtype)


def params():
    return pltpu.CompilerParams(vmem_limit_bytes=56 << 20)


def shards(feats, kmap, send_rows, w_sub, owner, coarse_id, octant, w_down, grad_coarse):
    chans, vdev = feats.shape
    _, levels, halo = send_rows.shape
    kvol = kmap.shape[0]
    noct, c2, _ = w_down.shape
    coarse_dev = grad_coarse.shape[1]
    keys = noct * coarse_dev
    slots = vdev // 32
    bits_member = lax.axis_size("member").bit_length() - 1
    myself = lax.axis_index(("group", "member")).astype(I32).reshape(1)
    lane_pad = LANES - chans
    outgoing = send_rows.reshape(1, levels * halo)
    table_rows = vdev + levels * halo + SUB
    index = kmap.reshape(kvol, 1, vdev)

    w_pad = jnp.pad(w_sub, ((0, 0), (0, lane_pad), (0, lane_pad)))
    w_forward = w_pad.transpose(0, 2, 1).reshape(kvol * LANES, LANES)
    w_backward = w_pad.transpose(1, 0, 2).reshape(LANES, kvol * LANES)
    down_pad = jnp.pad(w_down, ((0, 0), (0, 0), (0, lane_pad)))

    prepared = pl.pallas_call(
        functools.partial(prepare_kernel, levels, coarse_dev=coarse_dev, slots=slots),
        in_specs=[pl.BlockSpec(memory_space=SMEM), smem_full((1, levels * halo))]
        + [vmem_full((1, vdev))] * 3
        + [vmem_full((chans, vdev))],
        out_specs=[vmem_full((halo + 2 * SUB, LANES))] * levels
        + [vmem_full((vdev, LANES))]
        + [vmem_full((1, vdev))] * 3,
        out_shape=[shape((halo + 2 * SUB, LANES), BF16)] * levels
        + [shape((vdev, LANES), F32)]
        + [shape((1, vdev), I32)] * 3,
        scratch_shapes=[pltpu.VMEM((levels * halo, LANES), F32)],
        compiler_params=params(),
        name="prepare",
    )(myself, outgoing, owner.reshape(1, vdev), coarse_id.reshape(1, vdev), octant.reshape(1, vdev), feats)
    messages = prepared[:levels]
    table, position, parent, own_key = prepared[levels:]
    received = [from_partner(messages[level], level, bits_member) for level in range(levels)]

    digits = jnp.stack([got[halo : halo + 2] for got in received]).astype(F32)
    got_keys = (digits[:, 0] * DIGIT + digits[:, 1]).astype(I32).reshape(1, levels * slots)

    grads = pl.pallas_call(
        functools.partial(parents_kernel, levels),
        in_specs=[smem_full((1, levels * slots)), vmem_full((coarse_dev, c2)), vmem_full((noct, c2, LANES))],
        out_specs=[vmem_full((slots, LANES))] * levels + [vmem_full((keys, LANES))],
        out_shape=[shape((slots, LANES), BF16)] * levels + [shape((keys, LANES), F32)],
        scratch_shapes=[pltpu.VMEM((keys + SUB, LANES), F32), pltpu.VMEM((levels * slots, LANES), F32)],
        compiler_params=params(),
        name="parents",
    )(got_keys, grad_coarse.T, down_pad)
    grad_pooled = grads[levels]
    returned = [from_partner(grads[level], level, bits_member) for level in range(levels)]

    gathered = pl.pallas_call(
        functools.partial(gather_kernel, levels, halo),
        grid=(kvol,),
        in_specs=[
            pl.BlockSpec((1, 1, vdev), lambda k: (k, 0, 0), memory_space=SMEM),
            vmem_full((vdev, LANES)),
        ]
        + [vmem_full((halo + 2 * SUB, LANES))] * levels,
        out_specs=pl.BlockSpec((vdev, LANES), lambda k: (0, k)),
        out_shape=shape((vdev, kvol * LANES), BF16),
        scratch_shapes=[pltpu.VMEM((table_rows, LANES), F32), pltpu.VMEM((256, LANES), F32)],
        compiler_params=params(),
        cost_estimate=pl.CostEstimate(flops=0, bytes_accessed=300_000_000, transcendentals=0),
        name="gather",
    )(index, table, *received)

    pre = jnp.dot(gathered, w_forward, preferred_element_type=F32)

    pools = 4
    middle = pl.pallas_call(
        functools.partial(middle_kernel, levels, tables=pools),
        in_specs=[smem_full((1, vdev))] * 3
        + [vmem_full((vdev, LANES)), vmem_full((keys, LANES))]
        + [vmem_full((slots, LANES))] * levels,
        out_specs=[vmem_full((vdev, LANES)), vmem_full((keys, LANES))] + [vmem_full((slots, LANES))] * levels,
        out_shape=[shape((vdev, LANES), BF16), shape((keys, LANES), F32)] + [shape((slots, LANES), BF16)] * levels,
        scratch_shapes=[
            pltpu.VMEM((keys + levels * slots, LANES), F32),
            pltpu.VMEM((vdev, LANES), F32),
            pltpu.VMEM((vdev, LANES), F32),
            pltpu.VMEM((levels * slots + SUB, LANES), F32),
        ]
        + [pltpu.VMEM((keys + SUB, LANES), F32)] * pools,
        compiler_params=params(),
        name="middle",
    )(parent, position, own_key, pre, grad_pooled, *returned)
    grad_pre, pool_part = middle[:2]
    came = [from_partner(middle[2 + level], level, bits_member) for level in range(levels)]

    grad_w = lax.dot_general(grad_pre, gathered, (((0,), (0,)), ((), ())), preferred_element_type=F32)
    grad_w = grad_w.reshape(LANES, kvol, LANES)[:chans, :, :chans].transpose(1, 0, 2)
    terms = jnp.dot(grad_pre, w_backward, preferred_element_type=F32)

    coarse_out, grad_down = pl.pallas_call(
        functools.partial(pool_kernel, levels),
        in_specs=[
            smem_full((1, levels * slots)),
            vmem_full((keys, LANES)),
            vmem_full((c2, coarse_dev)),
            vmem_full((noct, c2, LANES)),
        ]
        + [vmem_full((slots, LANES))] * levels,
        out_specs=[vmem_full((c2, coarse_dev)), vmem_full((noct, c2, chans))],
        out_shape=[shape((c2, coarse_dev), BF16), shape((noct, c2, chans), F32)],
        scratch_shapes=[pltpu.VMEM((levels * slots, LANES), F32)]
        + [pltpu.VMEM((keys + SUB, LANES), F32)] * pools,
        compiler_params=params(),
        name="pool",
    )(got_keys, pool_part, grad_coarse, down_pad, *came)

    grad_w, grad_down, terms = lax.optimization_barrier((grad_w, grad_down, terms))
    grad_w, grad_down = lax.psum((grad_w, grad_down), ("group", "member"))

    accumulators = 8
    scattered = pl.pallas_call(
        functools.partial(scatter_kernel, levels, halo),
        grid=(kvol,),
        in_specs=[
            pl.BlockSpec((1, 1, vdev), lambda k: (k, 0, 0), memory_space=SMEM),
            pl.BlockSpec((vdev, LANES), lambda k: (0, k)),
        ],
        out_specs=[vmem_full((vdev, LANES))] + [vmem_full((halo, LANES))] * levels,
        out_shape=[shape((vdev, LANES), F32)] + [shape((halo, LANES), BF16)] * levels,
        scratch_shapes=[pltpu.VMEM((table_rows, LANES), F32)] * accumulators,
        compiler_params=params(),
        cost_estimate=pl.CostEstimate(flops=0, bytes_accessed=400_000_000, transcendentals=0),
        name="scatter",
    )(index, terms)
    incoming = [from_partner(scattered[1 + level], level, bits_member) for level in range(levels)]

    grad_feats = pl.pallas_call(
        functools.partial(finish_kernel, levels),
        in_specs=[smem_full((1, levels * halo)), vmem_full((vdev, LANES))] + [vmem_full((halo, LANES))] * levels,
        out_specs=vmem_full((chans, vdev)),
        out_shape=shape((chans, vdev), F32),
        scratch_shapes=[pltpu.VMEM((levels * halo, LANES), F32)] + [pltpu.VMEM((vdev, LANES), F32)] * 4,
        compiler_params=params(),
        name="finish",
    )(outgoing, scattered[0], *incoming)
    return coarse_out, grad_feats, grad_w, grad_down


def solution(mesh):
    both = ("group", "member")
    in_specs = (
        P(None, both),
        P(None, both),
        P(both, None, None),
        P(),
        P(both, None),
        P(both),
        P(both),
        P(),
        P(None, both),
    )
    out_specs = (P(None, both), P(None, both), P(), P())
    return jax.shard_map(shards, mesh=mesh, in_specs=in_specs, out_specs=out_specs, check_vma=False)
```

```python
import functools

import jax
import jax.numpy as jnp
from jax import lax
from jax.experimental import pallas as pl
from jax.experimental.pallas import tpu as pltpu
from jax.sharding import PartitionSpec as P

LANES = 128
SUB = 8
DIGIT = 64
SMEM = pltpu.SMEM
F32 = jnp.float32
BF16 = jnp.bfloat16
I32 = jnp.int32


def from_partner(value, level, bits_member):
    axis, stride = ("member", level) if level < bits_member else ("group", level - bits_member)
    mask = 2**stride
    pairs = [(source, source ^ mask) for source in range(lax.axis_size(axis))]
    return lax.ppermute(value, axis, pairs)


def vmem_full(shape):
    return pl.BlockSpec(shape, lambda *_: (0,) * len(shape))


def smem_full(shape):
    return pl.BlockSpec(shape, lambda *_: (0,) * len(shape), memory_space=SMEM)


def copy_rows(count, unroll, index, source, target):
    def body(step, _):
        base = pl.multiple_of(step * unroll, unroll)
        for j in range(unroll):
            target[pl.ds(base + j, 1), :] = source[pl.ds(index(base + j), 1), :]
        return 0

    lax.fori_loop(0, count // unroll, body, 0)


def add_rows(count, unroll, index, source, tables):
    lanes = len(tables)

    def body(step, _):
        base = pl.multiple_of(step * unroll, unroll)
        for start in range(0, unroll, lanes):
            spots = [index(base + start + j) for j in range(lanes)]
            sums = [
                tables[j][pl.ds(spots[j], 1), :] + source[pl.ds(base + start + j, 1), :]
                for j in range(lanes)
            ]
            for j in range(lanes):
                tables[j][pl.ds(spots[j], 1), :] = sums[j]
        return 0

    lax.fori_loop(0, count // unroll, body, 0)


def prepare_kernel(levels, me_ref, rows_ref, owner_ref, coarse_ref, octant_ref, feats_ref, *refs, noct, coarse_dev, slots):
    messages = refs[:levels]
    table_ref, self_ref, list_ref, pos_ref, buf = refs[levels:]
    chans, vdev = feats_ref.shape
    halo = rows_ref.shape[1] // levels
    noct_keys = noct * coarse_dev
    fill = jnp.zeros((LANES - chans, LANES), F32)
    for c in range(vdev // LANES):
        cols = pl.ds(c * LANES, LANES)
        block = jnp.concatenate([feats_ref[:, cols].astype(F32), fill], axis=0)
        table_ref[cols, :] = block.T
    copy_rows(levels * halo, 64, lambda r: rows_ref[0, r], table_ref, buf)

    differ = jnp.bitwise_xor(owner_ref[...], me_ref[0])
    level_id = lax.broadcasted_iota(I32, (SUB, LANES), 0)
    bit = jnp.where(level_id < levels, jnp.left_shift(jnp.ones_like(level_id), level_id), 0)
    chunks = vdev // LANES
    classes = []
    for c in range(chunks):
        part = jnp.broadcast_to(differ[:, c * LANES : (c + 1) * LANES], (SUB, LANES))
        classes.append(jnp.where((part == bit) & (level_id < levels), 1.0, 0.0).astype(F32))
    upper = lax.broadcasted_iota(I32, (LANES, LANES), 0) <= lax.broadcasted_iota(I32, (LANES, LANES), 1)
    prefix = jnp.dot(
        jnp.concatenate(classes, axis=0).astype(BF16),
        jnp.where(upper, 1.0, 0.0).astype(BF16),
        preferred_element_type=F32,
    )
    carry = jnp.zeros((SUB, 1), F32)
    start = (level_id * slots).astype(F32)
    digit_rows = []
    digit_id = lax.broadcasted_iota(I32, (SUB, LANES), 0)
    for c in range(chunks):
        cols = pl.ds(c * LANES, LANES)
        inclusive = prefix[c * SUB : (c + 1) * SUB]
        spot = classes[c] * (start + inclusive - 1.0 + carry)
        carry = carry + inclusive[:, LANES - 1 :]
        remote = jnp.sum(classes[c], axis=0, keepdims=True) > 0.5
        position = jnp.where(remote, jnp.sum(spot, axis=0, keepdims=True).astype(I32), levels * slots)
        keys = octant_ref[:, cols] * coarse_dev + coarse_ref[:, cols]
        pos_ref[:, cols] = position
        self_ref[:, cols] = jnp.where(remote, noct_keys, keys)
        voxel = lax.broadcasted_iota(I32, (SUB, LANES), 1) + c * LANES
        number = jnp.where(digit_id < 2, jnp.broadcast_to(keys, (SUB, LANES)), voxel)
        high = lax.shift_right_logical(number, 6) - DIGIT
        low = number & (DIGIT - 1)
        digits = jnp.where(digit_id < 4, jnp.where((digit_id & 1) == 0, high, low), 0)
        digit_rows.append(digits.astype(F32).astype(BF16))
    digits = jnp.concatenate(digit_rows, axis=1)
    slot_id = lax.broadcasted_iota(I32, (slots, LANES), 0)
    for level in range(levels):
        hot = []
        for c in range(chunks):
            position = jnp.broadcast_to(pos_ref[:, pl.ds(c * LANES, LANES)], (slots, LANES))
            hot.append(jnp.where(position == slot_id + level * slots, 1.0, 0.0).astype(BF16))
        found = lax.dot_general(
            digits, jnp.concatenate(hot, axis=1), (((1,), (1,)), ((), ())), preferred_element_type=F32
        )
        found = found + jnp.where((digit_id & 1) == 0, float(DIGIT), 0.0)
        list_ref[:, pl.ds(level * slots, slots)] = (found[2:3] * float(DIGIT) + found[3:4]).astype(I32)
        messages[level][pl.ds(0, halo), :] = buf[pl.ds(level * halo, halo), :].astype(BF16)
        messages[level][pl.ds(halo, 2 * SUB), :] = jnp.concatenate(
            [found, jnp.zeros((SUB, LANES), F32)], axis=0
        ).astype(BF16)


def parents_kernel(self_ref, coarse_ref, weight_ref, wide_ref, rows_ref):
    noct = weight_ref.shape[0]
    ndev = coarse_ref.shape[0]
    for o in range(noct):
        grad = jnp.dot(coarse_ref[...], weight_ref[o], preferred_element_type=F32)
        wide_ref[pl.ds(o * ndev, ndev), :] = grad.astype(BF16).astype(F32)
    wide_ref[pl.ds(noct * ndev, SUB), :] = jnp.zeros((SUB, LANES), F32)
    copy_rows(rows_ref.shape[0], 64, lambda r: self_ref[0, r], wide_ref, rows_ref)


def answer_kernel(levels, keys_ref, wide_ref, *refs):
    outs = refs[:levels]
    buf = refs[levels]
    slots = outs[0].shape[0]
    copy_rows(levels * slots, 64, lambda r: keys_ref[0, r], wide_ref, buf)
    for level in range(levels):
        outs[level][...] = buf[pl.ds(level * slots, slots), :].astype(BF16)


def index_copy(index_ref, spot, piece, store, sem, width):
    pieces = index_ref.shape[2] // width
    row = lax.div(piece, pieces)
    start = pl.multiple_of(lax.rem(piece, pieces) * width, width)
    return pltpu.make_async_copy(index_ref.at[row, :, pl.ds(start, width)], store, sem)


def walk(index_ref, stores, sems, vdev, chunk, step_of):
    k = pl.program_id(0)
    total = pl.num_programs(0)
    width = stores[0].shape[1]
    many = len(stores)
    pieces = vdev // width

    @pl.when(k == 0)
    def _():
        for b in range(many):
            index_copy(index_ref, b, b, stores[b], sems.at[b], width).start()

    def body(turn, _):
        for b in range(many):
            piece = k * pieces + turn * many + b
            index_copy(index_ref, b, piece, stores[b], sems.at[b], width).wait()
            for sub in range(width // chunk):
                base = pl.multiple_of((turn * many + b) * width + sub * chunk, chunk)
                step_of(base, sub % 2, stores[b], sub * chunk, b == 0 and sub == 0, turn)

            @pl.when(piece + many < total * pieces)
            def _():
                index_copy(index_ref, b, piece + many, stores[b], sems.at[b], width).start()

        return 0

    lax.fori_loop(0, pieces // many, body, 0)


def gather_kernel(levels, halo, index_ref, local_ref, weight_ref, *refs):
    received = refs[:levels]
    out_ref, pre_ref, table, buf0, buf1 = refs[levels : levels + 5]
    stores = refs[levels + 5 : -1]
    sems = refs[-1]
    bufs = (buf0, buf1)
    vdev = local_ref.shape[0]
    chunk = buf0.shape[0]

    @pl.when(pl.program_id(0) == 0)
    def _():
        table[pl.ds(0, vdev), :] = local_ref[...]
        for level in range(levels):
            table[pl.ds(vdev + level * halo, halo), :] = received[level][pl.ds(0, halo), :].astype(F32)
        table[pl.ds(vdev + levels * halo, SUB), :] = jnp.zeros((SUB, LANES), F32)
        pre_ref[...] = jnp.zeros_like(pre_ref)
        buf1[...] = jnp.zeros_like(buf1)

    def use(buf, base, live):
        taken = buf[...].astype(BF16)
        part = pl.ds(base, chunk)
        out_ref[part, :] = taken
        term = jnp.dot(taken, weight_ref[0], preferred_element_type=F32)
        if live is not None:
            term = term * live
        pre_ref[part, :] += term

    def step(base, parity, store, entry, first, turn):
        buf = bufs[parity]
        for j in range(chunk):
            buf[pl.ds(j, 1), :] = table[pl.ds(store[0, entry + j], 1), :]
        if first:
            behind = pl.multiple_of(jnp.maximum(base - chunk, 0), chunk)
            use(bufs[1 - parity], behind, jnp.minimum(turn, 1).astype(F32))
        else:
            use(bufs[1 - parity], pl.multiple_of(base - chunk, chunk), None)

    walk(index_ref, stores, sems, vdev, chunk, step)
    use(buf1, vdev - chunk, None)


def middle_kernel(levels, list_ref, pre_ref, rows_ref, *refs):
    returned = refs[:levels]
    grad_ref, turned_ref, act_ref = refs[levels : levels + 3]
    sends = refs[levels + 3 : 2 * levels + 3]
    rows, back, act, out = refs[2 * levels + 3 :]
    vdev = pre_ref.shape[0]
    slots = returned[0].shape[0]
    rows[pl.ds(0, vdev), :] = rows_ref[...]
    for level in range(levels):
        back[pl.ds(level * slots, slots), :] = returned[level][...].astype(F32)

    def patch(step, _):
        base = pl.multiple_of(step * 64, 64)
        for j in range(64):
            rows[pl.ds(list_ref[0, base + j], 1), :] = back[pl.ds(base + j, 1), :]
        return 0

    lax.fori_loop(0, levels * slots // 64, patch, 0)

    for step in range(vdev // LANES):
        part = pl.ds(step * LANES, LANES)
        pre = pre_ref[part, :]
        sig = 1.0 / (1.0 + jnp.exp(-pre))
        value = (pre * sig).astype(BF16).astype(F32)
        act[part, :] = value
        act_ref[part, :] = value
        grad = rows[part, :] * (sig * (1.0 + pre * (1.0 - sig)))
        grad_ref[part, :] = grad.astype(BF16)
        turned_ref[:, part] = grad.T.astype(BF16)
    act[pl.ds(vdev, SUB), :] = jnp.zeros((SUB, LANES), F32)
    copy_rows(levels * slots, 64, lambda r: list_ref[0, r], act, out)
    for level in range(levels):
        sends[level][...] = out[pl.ds(level * slots, slots), :].astype(BF16)


def weights_kernel(turned_ref, taken_ref, out_ref):
    wide = jnp.dot(turned_ref[...], taken_ref[...], preferred_element_type=F32)
    many, rows, cols = out_ref.shape
    for j in range(many):
        out_ref[j] = wide[:rows, j * LANES : j * LANES + cols]


def pool_kernel(levels, keys_ref, self_ref, act_ref, grad_ref, weight_ref, *refs):
    received = refs[:levels]
    coarse_ref, down_ref, rows = refs[levels : levels + 3]
    pools = refs[levels + 3 :]
    slots = received[0].shape[0]
    noct, _, chans = down_ref.shape
    ndev = grad_ref.shape[1]
    for level in range(levels):
        rows[pl.ds(level * slots, slots), :] = received[level][...].astype(F32)
    for pool in pools:
        pool[...] = jnp.zeros_like(pool)
    add_rows(act_ref.shape[0], 64, lambda r: self_ref[0, r], act_ref, pools)
    add_rows(levels * slots, 64, lambda r: keys_ref[0, r], rows, pools)
    coarse = jnp.zeros(coarse_ref.shape, F32)
    for o in range(noct):
        part = pl.ds(o * ndev, ndev)
        total = pools[0][part, :]
        for pool in pools[1:]:
            total = total + pool[part, :]
        pooled = total.astype(BF16)
        coarse = coarse + lax.dot_general(
            weight_ref[o], pooled, (((1,), (1,)), ((), ())), preferred_element_type=F32
        )
        down = jnp.dot(grad_ref[...], pooled, preferred_element_type=F32)
        down_ref[o] = down[:, :chans]
    coarse_ref[...] = coarse.astype(BF16)


def scatter_kernel(levels, halo, stages, index_ref, grad_ref, weight_ref, local_ref, *refs):
    backs = refs[:levels]
    buf0, buf1 = refs[levels : levels + 2]
    stores = refs[levels + 2 : levels + 2 + stages]
    tables = refs[levels + 2 + stages : -1]
    sems = refs[-1]
    bufs = (buf0, buf1)
    vdev = local_ref.shape[0]
    chunk = buf0.shape[0]
    lanes = len(tables)
    k = pl.program_id(0)
    last = pl.num_programs(0) - 1

    def ready(base, offset, buf):
        buf[...] = jnp.dot(grad_ref[pl.ds(base, chunk), :], weight_ref[offset], preferred_element_type=F32)

    @pl.when(k == 0)
    def _():
        for table in tables:
            table[...] = jnp.zeros_like(table)
        ready(0, 0, buf0)

    def step(base, parity, store, entry, first, turn):
        buf = bufs[parity]
        over = base + chunk == vdev
        ahead = pl.multiple_of(jnp.where(over, 0, base + chunk), chunk)
        ready(ahead, jnp.minimum(jnp.where(over, k + 1, k), last), bufs[1 - parity])
        for start in range(0, chunk, lanes):
            spots = [store[0, entry + start + j] for j in range(lanes)]
            sums = [tables[j][pl.ds(spots[j], 1), :] + buf[pl.ds(start + j, 1), :] for j in range(lanes)]
            for j in range(lanes):
                tables[j][pl.ds(spots[j], 1), :] = sums[j]

    walk(index_ref, stores, sems, vdev, chunk, step)

    @pl.when(k == last)
    def _():
        def total(part):
            result = tables[0][part, :]
            for table in tables[1:]:
                result = result + table[part, :]
            return result

        local_ref[...] = total(pl.ds(0, vdev))
        for level in range(levels):
            backs[level][...] = total(pl.ds(vdev + level * halo, halo)).astype(BF16)


def finish_kernel(levels, rows_ref, local_ref, *refs):
    incoming = refs[:levels]
    out_ref, rows = refs[levels : levels + 2]
    tables = refs[levels + 2 :]
    halo = incoming[0].shape[0]
    chans, vdev = out_ref.shape
    for level in range(levels):
        rows[pl.ds(level * halo, halo), :] = incoming[level][...].astype(F32)
    for table in tables:
        table[...] = jnp.zeros_like(table)
    add_rows(levels * halo, 64, lambda r: rows_ref[0, r], rows, tables)
    for c in range(vdev // LANES):
        part = pl.ds(c * LANES, LANES)
        total = local_ref[part, :]
        for table in tables:
            total = total + table[part, :]
        out_ref[:, part] = total.T[:chans]


def shape(dims, dtype):
    return jax.ShapeDtypeStruct(dims, dtype)


def params():
    return pltpu.CompilerParams(vmem_limit_bytes=56 << 20)


def shards(feats, kmap, send_rows, w_sub, owner, coarse_id, octant, w_down, grad_coarse):
    chans, vdev = feats.shape
    _, levels, halo = send_rows.shape
    kvol = kmap.shape[0]
    noct, c2, _ = w_down.shape
    coarse_dev = grad_coarse.shape[1]
    keys = noct * coarse_dev
    slots = vdev // 32
    bits_member = lax.axis_size("member").bit_length() - 1
    myself = lax.axis_index(("group", "member")).astype(I32).reshape(1)
    lane_pad = LANES - chans
    outgoing = send_rows.reshape(1, levels * halo)
    table_rows = vdev + levels * halo + SUB
    index = kmap.reshape(kvol, 1, vdev)

    w_backward = jnp.pad(w_sub, ((0, 0), (0, lane_pad), (0, lane_pad)))
    w_forward = w_backward.transpose(0, 2, 1)
    down_pad = jnp.pad(w_down, ((0, 0), (0, 0), (0, lane_pad)))

    prepared = pl.pallas_call(
        functools.partial(prepare_kernel, levels, noct=noct, coarse_dev=coarse_dev, slots=slots),
        in_specs=[pl.BlockSpec(memory_space=SMEM), smem_full((1, levels * halo))]
        + [vmem_full((1, vdev))] * 3
        + [vmem_full((chans, vdev))],
        out_specs=[vmem_full((halo + 2 * SUB, LANES))] * levels
        + [vmem_full((vdev, LANES)), vmem_full((1, vdev)), vmem_full((1, levels * slots))],
        out_shape=[shape((halo + 2 * SUB, LANES), BF16)] * levels
        + [shape((vdev, LANES), F32), shape((1, vdev), I32), shape((1, levels * slots), I32)],
        scratch_shapes=[pltpu.VMEM((1, vdev), I32), pltpu.VMEM((levels * halo, LANES), F32)],
        compiler_params=params(),
        name="prepare",
    )(myself, outgoing, owner.reshape(1, vdev), coarse_id.reshape(1, vdev), octant.reshape(1, vdev), feats)
    messages = prepared[:levels]
    table, own_key, send_list = prepared[levels:]
    received = [from_partner(messages[level], level, bits_member) for level in range(levels)]

    wide, rows = pl.pallas_call(
        parents_kernel,
        in_specs=[smem_full((1, vdev)), vmem_full((coarse_dev, c2)), vmem_full((noct, c2, LANES))],
        out_specs=[vmem_full((keys + SUB, LANES)), vmem_full((vdev, LANES))],
        out_shape=[shape((keys + SUB, LANES), F32), shape((vdev, LANES), F32)],
        compiler_params=params(),
        name="parents",
    )(own_key, grad_coarse.T, down_pad)

    digits = jnp.stack([got[halo : halo + 2] for got in received]).astype(F32)
    got_keys = (digits[:, 0] * DIGIT + digits[:, 1]).astype(I32).reshape(1, levels * slots)
    answers = pl.pallas_call(
        functools.partial(answer_kernel, levels),
        in_specs=[smem_full((1, levels * slots)), vmem_full((keys + SUB, LANES))],
        out_specs=[vmem_full((slots, LANES))] * levels,
        out_shape=[shape((slots, LANES), BF16)] * levels,
        scratch_shapes=[pltpu.VMEM((levels * slots, LANES), F32)],
        compiler_params=params(),
        name="answer",
    )(got_keys, wide)
    returned = [from_partner(answers[level], level, bits_member) for level in range(levels)]

    stages, width, chunk = 4, 512, 256
    staging = [pltpu.SMEM((1, width), I32)] * stages
    gathered, pre = pl.pallas_call(
        functools.partial(gather_kernel, levels, halo),
        grid=(kvol,),
        in_specs=[
            pl.BlockSpec(memory_space=pl.ANY),
            vmem_full((vdev, LANES)),
            pl.BlockSpec((1, LANES, LANES), lambda k: (k, 0, 0)),
        ]
        + [vmem_full((halo + 2 * SUB, LANES))] * levels,
        out_specs=[pl.BlockSpec((vdev, LANES), lambda k: (0, k)), vmem_full((vdev, LANES))],
        out_shape=[shape((vdev, kvol * LANES), BF16), shape((vdev, LANES), F32)],
        scratch_shapes=[pltpu.VMEM((table_rows, LANES), F32)]
        + [pltpu.VMEM((chunk, LANES), F32)] * 2
        + staging
        + [pltpu.SemaphoreType.DMA((stages,))],
        compiler_params=params(),
        cost_estimate=pl.CostEstimate(flops=0, bytes_accessed=300_000_000, transcendentals=0),
        name="gather",
    )(index, table, w_forward, *received)

    middle = pl.pallas_call(
        functools.partial(middle_kernel, levels),
        in_specs=[smem_full((1, levels * slots))]
        + [vmem_full((vdev, LANES))] * 2
        + [vmem_full((slots, LANES))] * levels,
        out_specs=[vmem_full((vdev, LANES)), vmem_full((LANES, vdev)), vmem_full((vdev, LANES))]
        + [vmem_full((slots, LANES))] * levels,
        out_shape=[shape((vdev, LANES), BF16), shape((LANES, vdev), BF16), shape((vdev, LANES), F32)]
        + [shape((slots, LANES), BF16)] * levels,
        scratch_shapes=[
            pltpu.VMEM((vdev + SUB, LANES), F32),
            pltpu.VMEM((levels * slots, LANES), F32),
            pltpu.VMEM((vdev + SUB, LANES), F32),
            pltpu.VMEM((levels * slots, LANES), F32),
        ],
        compiler_params=params(),
        name="middle",
    )(send_list, pre, rows, *returned)
    grad_pre, grad_turned, act = middle[:3]
    came = [from_partner(middle[3 + level], level, bits_member) for level in range(levels)]

    group = 3
    grad_w = pl.pallas_call(
        weights_kernel,
        grid=(kvol // group,),
        in_specs=[vmem_full((LANES, vdev)), pl.BlockSpec((vdev, group * LANES), lambda k: (0, k))],
        out_specs=pl.BlockSpec((group, chans, chans), lambda k: (k, 0, 0)),
        out_shape=shape((kvol, chans, chans), F32),
        compiler_params=params(),
        cost_estimate=pl.CostEstimate(flops=0, bytes_accessed=40_000_000, transcendentals=0),
        name="weights",
    )(grad_turned, gathered)

    coarse_out, grad_down = pl.pallas_call(
        functools.partial(pool_kernel, levels),
        in_specs=[
            smem_full((1, levels * slots)),
            smem_full((1, vdev)),
            vmem_full((vdev, LANES)),
            vmem_full((c2, coarse_dev)),
            vmem_full((noct, c2, LANES)),
        ]
        + [vmem_full((slots, LANES))] * levels,
        out_specs=[vmem_full((c2, coarse_dev)), vmem_full((noct, c2, chans))],
        out_shape=[shape((c2, coarse_dev), BF16), shape((noct, c2, chans), F32)],
        scratch_shapes=[pltpu.VMEM((levels * slots, LANES), F32)]
        + [pltpu.VMEM((keys + SUB, LANES), F32)] * 8,
        compiler_params=params(),
        name="pool",
    )(got_keys, own_key, act, grad_coarse, down_pad, *came)

    grad_w, grad_down, grad_pre = lax.optimization_barrier((grad_w, grad_down, grad_pre))
    grad_w, grad_down = lax.psum((grad_w, grad_down), ("group", "member"))

    accumulators = 8
    scattered = pl.pallas_call(
        functools.partial(scatter_kernel, levels, halo, stages),
        grid=(kvol,),
        in_specs=[
            pl.BlockSpec(memory_space=pl.ANY),
            vmem_full((vdev, LANES)),
            vmem_full((kvol, LANES, LANES)),
        ],
        out_specs=[vmem_full((vdev, LANES))] + [vmem_full((halo, LANES))] * levels,
        out_shape=[shape((vdev, LANES), F32)] + [shape((halo, LANES), BF16)] * levels,
        scratch_shapes=[pltpu.VMEM((chunk, LANES), F32)] * 2
        + staging
        + [pltpu.VMEM((table_rows, LANES), F32)] * accumulators
        + [pltpu.SemaphoreType.DMA((stages,))],
        compiler_params=params(),
        cost_estimate=pl.CostEstimate(flops=0, bytes_accessed=400_000_000, transcendentals=0),
        name="scatter",
    )(index, grad_pre, w_backward)
    incoming = [from_partner(scattered[1 + level], level, bits_member) for level in range(levels)]

    grad_feats = pl.pallas_call(
        functools.partial(finish_kernel, levels),
        in_specs=[smem_full((1, levels * halo)), vmem_full((vdev, LANES))] + [vmem_full((halo, LANES))] * levels,
        out_specs=vmem_full((chans, vdev)),
        out_shape=shape((chans, vdev), F32),
        scratch_shapes=[pltpu.VMEM((levels * halo, LANES), F32)] + [pltpu.VMEM((vdev, LANES), F32)] * 4,
        compiler_params=params(),
        name="finish",
    )(outgoing, scattered[0], *incoming)
    return coarse_out, grad_feats, grad_w, grad_down


def solution(mesh):
    both = ("group", "member")
    in_specs = (
        P(None, both),
        P(None, both),
        P(both, None, None),
        P(),
        P(both, None),
        P(both),
        P(both),
        P(),
        P(None, both),
    )
    out_specs = (P(None, both), P(None, both), P(), P())
    return jax.shard_map(shards, mesh=mesh, in_specs=in_specs, out_specs=out_specs, check_vma=False)
```

```python
import functools

import jax
import jax.numpy as jnp
from jax import lax
from jax.experimental import pallas as pl
from jax.experimental.pallas import tpu as pltpu
from jax.sharding import PartitionSpec as P

LANES = 128
SUB = 8
DIGIT = 64
SMEM = pltpu.SMEM
F32 = jnp.float32
BF16 = jnp.bfloat16
I32 = jnp.int32


def from_partner(value, level, bits_member):
    axis, stride = ("member", level) if level < bits_member else ("group", level - bits_member)
    mask = 2**stride
    pairs = [(source, source ^ mask) for source in range(lax.axis_size(axis))]
    return lax.ppermute(value, axis, pairs)


def vmem_full(shape):
    return pl.BlockSpec(shape, lambda *_: (0,) * len(shape))


def smem_full(shape):
    return pl.BlockSpec(shape, lambda *_: (0,) * len(shape), memory_space=SMEM)


def copy_rows(count, unroll, index, source, target):
    def body(step, _):
        base = pl.multiple_of(step * unroll, unroll)
        for j in range(unroll):
            target[pl.ds(base + j, 1), :] = source[pl.ds(index(base + j), 1), :]
        return 0

    lax.fori_loop(0, count // unroll, body, 0)


def add_rows(count, unroll, index, source, tables):
    lanes = len(tables)

    def body(step, _):
        base = pl.multiple_of(step * unroll, unroll)
        for start in range(0, unroll, lanes):
            spots = [index(base + start + j) for j in range(lanes)]
            sums = [
                tables[j][pl.ds(spots[j], 1), :] + source[pl.ds(base + start + j, 1), :]
                for j in range(lanes)
            ]
            for j in range(lanes):
                tables[j][pl.ds(spots[j], 1), :] = sums[j]
        return 0

    lax.fori_loop(0, count // unroll, body, 0)


def prepare_kernel(levels, me_ref, rows_ref, owner_ref, coarse_ref, octant_ref, feats_ref, *refs, noct, coarse_dev, slots):
    messages = refs[:levels]
    table_ref, self_ref, list_ref, pos_ref, buf = refs[levels:]
    chans, vdev = feats_ref.shape
    halo = rows_ref.shape[1] // levels
    noct_keys = noct * coarse_dev
    fill = jnp.zeros((LANES - chans, LANES), F32)
    for c in range(vdev // LANES):
        cols = pl.ds(c * LANES, LANES)
        block = jnp.concatenate([feats_ref[:, cols].astype(F32), fill], axis=0)
        table_ref[cols, :] = block.T
    copy_rows(levels * halo, 64, lambda r: rows_ref[0, r], table_ref, buf)

    differ = jnp.bitwise_xor(owner_ref[...], me_ref[0])
    level_id = lax.broadcasted_iota(I32, (SUB, LANES), 0)
    bit = jnp.where(level_id < levels, jnp.left_shift(jnp.ones_like(level_id), level_id), 0)
    chunks = vdev // LANES
    classes = []
    for c in range(chunks):
        part = jnp.broadcast_to(differ[:, c * LANES : (c + 1) * LANES], (SUB, LANES))
        classes.append(jnp.where((part == bit) & (level_id < levels), 1.0, 0.0).astype(F32))
    upper = lax.broadcasted_iota(I32, (LANES, LANES), 0) <= lax.broadcasted_iota(I32, (LANES, LANES), 1)
    prefix = jnp.dot(
        jnp.concatenate(classes, axis=0).astype(BF16),
        jnp.where(upper, 1.0, 0.0).astype(BF16),
        preferred_element_type=F32,
    )
    carry = jnp.zeros((SUB, 1), F32)
    start = (level_id * slots).astype(F32)
    digit_rows = []
    digit_id = lax.broadcasted_iota(I32, (SUB, LANES), 0)
    for c in range(chunks):
        cols = pl.ds(c * LANES, LANES)
        inclusive = prefix[c * SUB : (c + 1) * SUB]
        spot = classes[c] * (start + inclusive - 1.0 + carry)
        carry = carry + inclusive[:, LANES - 1 :]
        remote = jnp.sum(classes[c], axis=0, keepdims=True) > 0.5
        position = jnp.where(remote, jnp.sum(spot, axis=0, keepdims=True).astype(I32), levels * slots)
        keys = octant_ref[:, cols] * coarse_dev + coarse_ref[:, cols]
        pos_ref[:, cols] = position
        self_ref[:, cols] = jnp.where(remote, noct_keys, keys)
        voxel = lax.broadcasted_iota(I32, (SUB, LANES), 1) + c * LANES
        number = jnp.where(digit_id < 2, jnp.broadcast_to(keys, (SUB, LANES)), voxel)
        high = lax.shift_right_logical(number, 6) - DIGIT
        low = number & (DIGIT - 1)
        digits = jnp.where(digit_id < 4, jnp.where((digit_id & 1) == 0, high, low), 0)
        digit_rows.append(digits.astype(F32).astype(BF16))
    digits = jnp.concatenate(digit_rows, axis=1)
    slot_id = lax.broadcasted_iota(I32, (slots, LANES), 0)
    for level in range(levels):
        hot = []
        for c in range(chunks):
            position = jnp.broadcast_to(pos_ref[:, pl.ds(c * LANES, LANES)], (slots, LANES))
            hot.append(jnp.where(position == slot_id + level * slots, 1.0, 0.0).astype(BF16))
        found = lax.dot_general(
            digits, jnp.concatenate(hot, axis=1), (((1,), (1,)), ((), ())), preferred_element_type=F32
        )
        found = found + jnp.where((digit_id & 1) == 0, float(DIGIT), 0.0)
        list_ref[:, pl.ds(level * slots, slots)] = (found[2:3] * float(DIGIT) + found[3:4]).astype(I32)
        messages[level][pl.ds(0, halo), :] = buf[pl.ds(level * halo, halo), :].astype(BF16)
        messages[level][pl.ds(halo, 2 * SUB), :] = jnp.concatenate(
            [found, jnp.zeros((SUB, LANES), F32)], axis=0
        ).astype(BF16)


def parents_kernel(self_ref, coarse_ref, weight_ref, wide_ref, rows_ref):
    noct = weight_ref.shape[0]
    ndev = coarse_ref.shape[0]
    for o in range(noct):
        grad = jnp.dot(coarse_ref[...], weight_ref[o], preferred_element_type=F32)
        wide_ref[pl.ds(o * ndev, ndev), :] = grad.astype(BF16).astype(F32)
    wide_ref[pl.ds(noct * ndev, SUB), :] = jnp.zeros((SUB, LANES), F32)
    copy_rows(rows_ref.shape[0], 64, lambda r: self_ref[0, r], wide_ref, rows_ref)


def answer_kernel(levels, keys_ref, wide_ref, *refs):
    outs = refs[:levels]
    buf = refs[levels]
    slots = outs[0].shape[0]
    copy_rows(levels * slots, 64, lambda r: keys_ref[0, r], wide_ref, buf)
    for level in range(levels):
        outs[level][...] = buf[pl.ds(level * slots, slots), :].astype(BF16)


def index_copy(index_ref, piece, store, sem, width):
    pieces = index_ref.shape[2] // width
    row = lax.div(piece, pieces)
    start = pl.multiple_of(lax.rem(piece, pieces) * width, width)
    return pltpu.make_async_copy(index_ref.at[row, :, pl.ds(start, width)], store, sem)


def walk(index_ref, stores, sems, vdev, chunk, step_of):
    k = pl.program_id(0)
    total = pl.num_programs(0)
    width = stores[0].shape[1]
    many = len(stores)
    pieces = vdev // width

    @pl.when(k == 0)
    def _():
        for b in range(many):
            index_copy(index_ref, b, stores[b], sems.at[b], width).start()

    def body(turn, _):
        for b in range(many):
            piece = k * pieces + turn * many + b
            index_copy(index_ref, piece, stores[b], sems.at[b], width).wait()
            for sub in range(width // chunk):
                base = pl.multiple_of((turn * many + b) * width + sub * chunk, chunk)
                step_of(base, (b * (width // chunk) + sub) % 2, stores[b], sub * chunk)

            @pl.when(piece + many < total * pieces)
            def _():
                index_copy(index_ref, piece + many, stores[b], sems.at[b], width).start()

        return 0

    lax.fori_loop(0, pieces // many, body, 0)


def gather_kernel(levels, halo, index_ref, local_ref, *refs):
    received = refs[:levels]
    out_ref, table, buf0, buf1 = refs[levels : levels + 4]
    stores = refs[levels + 4 : -1]
    sems = refs[-1]
    bufs = (buf0, buf1)
    vdev = local_ref.shape[0]
    chunk = buf0.shape[0]

    @pl.when(pl.program_id(0) == 0)
    def _():
        table[pl.ds(0, vdev), :] = local_ref[...]
        for level in range(levels):
            table[pl.ds(vdev + level * halo, halo), :] = received[level][pl.ds(0, halo), :].astype(F32)
        table[pl.ds(vdev + levels * halo, SUB), :] = jnp.zeros((SUB, LANES), F32)
        buf1[...] = jnp.zeros_like(buf1)

    def step(base, parity, store, entry):
        buf = bufs[parity]
        for j in range(chunk):
            buf[pl.ds(j, 1), :] = table[pl.ds(store[0, entry + j], 1), :]
        behind = pl.multiple_of(jnp.maximum(base - chunk, 0), chunk)
        out_ref[pl.ds(behind, chunk), :] = bufs[1 - parity][...].astype(BF16)

    walk(index_ref, stores, sems, vdev, chunk, step)
    out_ref[pl.ds(vdev - chunk, chunk), :] = buf1[...].astype(BF16)


def middle_kernel(levels, list_ref, pre_ref, rows_ref, *refs):
    returned = refs[:levels]
    grad_ref, turned_ref, act_ref = refs[levels : levels + 3]
    sends = refs[levels + 3 : 2 * levels + 3]
    rows, back, act, out = refs[2 * levels + 3 :]
    vdev = pre_ref.shape[0]
    slots = returned[0].shape[0]
    rows[pl.ds(0, vdev), :] = rows_ref[...]
    for level in range(levels):
        back[pl.ds(level * slots, slots), :] = returned[level][...].astype(F32)

    def patch(step, _):
        base = pl.multiple_of(step * 64, 64)
        for j in range(64):
            rows[pl.ds(list_ref[0, base + j], 1), :] = back[pl.ds(base + j, 1), :]
        return 0

    lax.fori_loop(0, levels * slots // 64, patch, 0)

    for step in range(vdev // LANES):
        part = pl.ds(step * LANES, LANES)
        pre = pre_ref[part, :]
        sig = 1.0 / (1.0 + jnp.exp(-pre))
        value = (pre * sig).astype(BF16).astype(F32)
        act[part, :] = value
        act_ref[part, :] = value
        grad = rows[part, :] * (sig * (1.0 + pre * (1.0 - sig)))
        grad_ref[part, :] = grad.astype(BF16)
        turned_ref[:, part] = grad.T.astype(BF16)
    act[pl.ds(vdev, SUB), :] = jnp.zeros((SUB, LANES), F32)
    copy_rows(levels * slots, 64, lambda r: list_ref[0, r], act, out)
    for level in range(levels):
        sends[level][...] = out[pl.ds(level * slots, slots), :].astype(BF16)


def weights_kernel(turned_ref, taken_ref, out_ref):
    wide = jnp.dot(turned_ref[...], taken_ref[...], preferred_element_type=F32)
    many = wide.shape[1] // LANES
    rows = out_ref.shape[0] // many
    for j in range(many):
        out_ref[pl.ds(j * rows, rows), :] = wide[:rows, j * LANES : (j + 1) * LANES].astype(BF16)


def unpack_kernel(full_ref, weights_ref, down_ref):
    kvol, chans, _ = weights_ref.shape
    noct, c2, _ = down_ref.shape
    for k in range(kvol):
        weights_ref[k] = full_ref[pl.ds(k * chans, chans), :][:, :chans]
    first = kvol * chans
    rest = LANES - chans
    for o in range(noct - 1):
        down_ref[o] = full_ref[pl.ds(first + o * c2, c2), :][:, :chans]
    start = first + (noct - 1) * c2
    down_ref[noct - 1, pl.ds(0, c2 - rest), :] = full_ref[pl.ds(start, c2 - rest), :][:, :chans]
    lane = lax.broadcasted_iota(I32, (rest, LANES), 1)
    tail = jnp.zeros((rest, LANES), F32)
    for j in range(chans // rest):
        piece = pltpu.roll(full_ref[pl.ds(first + j * rest, rest), :], rest * (j + 1), 1)
        tail = jnp.where((lane >= j * rest) & (lane < (j + 1) * rest), piece, tail)
    down_ref[noct - 1, pl.ds(c2 - rest, rest), :] = tail[:, :chans]


def pool_kernel(levels, chans, keys_ref, self_ref, act_ref, grad_ref, weight_ref, *refs):
    received = refs[:levels]
    coarse_ref, down_ref, rows = refs[levels : levels + 3]
    pools = refs[levels + 3 :]
    slots = received[0].shape[0]
    noct, c2, _ = weight_ref.shape
    rest = LANES - chans
    ndev = grad_ref.shape[1]
    for level in range(levels):
        rows[pl.ds(level * slots, slots), :] = received[level][...].astype(F32)
    for pool in pools:
        pool[...] = jnp.zeros_like(pool)
    add_rows(act_ref.shape[0], 64, lambda r: self_ref[0, r], act_ref, pools)
    add_rows(levels * slots, 64, lambda r: keys_ref[0, r], rows, pools)
    coarse = jnp.zeros(coarse_ref.shape, F32)
    lane = lax.broadcasted_iota(I32, (rest, LANES), 1)
    for o in reversed(range(noct)):
        part = pl.ds(o * ndev, ndev)
        total = pools[0][part, :]
        for pool in pools[1:]:
            total = total + pool[part, :]
        pooled = total.astype(BF16)
        coarse = coarse + lax.dot_general(
            weight_ref[o], pooled, (((1,), (1,)), ((), ())), preferred_element_type=F32
        )
        down = jnp.dot(grad_ref[...], pooled, preferred_element_type=F32)
        if o == noct - 1:
            tail = down[c2 - rest :]
            down = down[: c2 - rest]
        if o == 0:
            parts = []
            for j in range(chans // rest):
                piece = pltpu.roll(tail, (chans - rest * j) % LANES, 1)
                parts.append(jnp.where(lane >= chans, piece, down[j * rest : (j + 1) * rest]))
            down = jnp.concatenate(parts + [down[chans:]], axis=0)
        down_ref[pl.ds(o * c2, down.shape[0]), :] = down.astype(BF16)
    coarse_ref[...] = coarse.astype(BF16)


def scatter_kernel(levels, halo, stages, index_ref, grad_ref, weight_ref, local_ref, *refs):
    backs = refs[:levels]
    buf0, buf1 = refs[levels : levels + 2]
    stores = refs[levels + 2 : levels + 2 + stages]
    tables = refs[levels + 2 + stages : -1]
    sems = refs[-1]
    bufs = (buf0, buf1)
    vdev = local_ref.shape[0]
    chunk = buf0.shape[0]
    lanes = len(tables)
    k = pl.program_id(0)
    last = pl.num_programs(0) - 1

    def ready(base, offset, buf):
        buf[...] = jnp.dot(grad_ref[pl.ds(base, chunk), :], weight_ref[offset], preferred_element_type=F32)

    @pl.when(k == 0)
    def _():
        for table in tables:
            table[...] = jnp.zeros_like(table)
        ready(0, 0, buf0)

    def step(base, parity, store, entry):
        buf = bufs[parity]
        over = base + chunk == vdev
        ahead = pl.multiple_of(jnp.where(over, 0, base + chunk), chunk)
        ready(ahead, jnp.minimum(jnp.where(over, k + 1, k), last), bufs[1 - parity])
        for start in range(0, chunk, lanes):
            spots = [store[0, entry + start + j] for j in range(lanes)]
            sums = [tables[j][pl.ds(spots[j], 1), :] + buf[pl.ds(start + j, 1), :] for j in range(lanes)]
            for j in range(lanes):
                tables[j][pl.ds(spots[j], 1), :] = sums[j]

    walk(index_ref, stores, sems, vdev, chunk, step)

    @pl.when(k == last)
    def _():
        def total(part):
            result = tables[0][part, :]
            for table in tables[1:]:
                result = result + table[part, :]
            return result

        local_ref[...] = total(pl.ds(0, vdev))
        for level in range(levels):
            backs[level][...] = total(pl.ds(vdev + level * halo, halo)).astype(BF16)


def finish_kernel(levels, rows_ref, local_ref, *refs):
    incoming = refs[:levels]
    out_ref, rows = refs[levels : levels + 2]
    tables = refs[levels + 2 :]
    halo = incoming[0].shape[0]
    chans, vdev = out_ref.shape
    for level in range(levels):
        rows[pl.ds(level * halo, halo), :] = incoming[level][...].astype(F32)
    for table in tables:
        table[...] = jnp.zeros_like(table)
    add_rows(levels * halo, 64, lambda r: rows_ref[0, r], rows, tables)
    for c in range(vdev // LANES):
        part = pl.ds(c * LANES, LANES)
        total = local_ref[part, :]
        for table in tables:
            total = total + table[part, :]
        out_ref[:, part] = total.T[:chans]


def shape(dims, dtype):
    return jax.ShapeDtypeStruct(dims, dtype)


def params():
    return pltpu.CompilerParams(vmem_limit_bytes=56 << 20)


def shards(feats, kmap, send_rows, w_sub, owner, coarse_id, octant, w_down, grad_coarse):
    chans, vdev = feats.shape
    _, levels, halo = send_rows.shape
    kvol = kmap.shape[0]
    noct, c2, _ = w_down.shape
    coarse_dev = grad_coarse.shape[1]
    keys = noct * coarse_dev
    slots = vdev // 32
    bits_member = lax.axis_size("member").bit_length() - 1
    myself = lax.axis_index(("group", "member")).astype(I32).reshape(1)
    lane_pad = LANES - chans
    outgoing = send_rows.reshape(1, levels * halo)
    table_rows = vdev + levels * halo + SUB
    index = kmap.reshape(kvol, 1, vdev)

    w_backward = jnp.pad(w_sub, ((0, 0), (0, lane_pad), (0, lane_pad)))
    w_forward = w_backward.transpose(0, 2, 1).reshape(kvol * LANES, LANES)
    down_pad = jnp.pad(w_down, ((0, 0), (0, 0), (0, lane_pad)))

    prepared = pl.pallas_call(
        functools.partial(prepare_kernel, levels, noct=noct, coarse_dev=coarse_dev, slots=slots),
        in_specs=[pl.BlockSpec(memory_space=SMEM), smem_full((1, levels * halo))]
        + [vmem_full((1, vdev))] * 3
        + [vmem_full((chans, vdev))],
        out_specs=[vmem_full((halo + 2 * SUB, LANES))] * levels
        + [vmem_full((vdev, LANES)), vmem_full((1, vdev)), vmem_full((1, levels * slots))],
        out_shape=[shape((halo + 2 * SUB, LANES), BF16)] * levels
        + [shape((vdev, LANES), F32), shape((1, vdev), I32), shape((1, levels * slots), I32)],
        scratch_shapes=[pltpu.VMEM((1, vdev), I32), pltpu.VMEM((levels * halo, LANES), F32)],
        compiler_params=params(),
        name="prepare",
    )(myself, outgoing, owner.reshape(1, vdev), coarse_id.reshape(1, vdev), octant.reshape(1, vdev), feats)
    messages = prepared[:levels]
    table, own_key, send_list = prepared[levels:]
    received = [from_partner(messages[level], level, bits_member) for level in range(levels)]

    wide, rows = pl.pallas_call(
        parents_kernel,
        in_specs=[smem_full((1, vdev)), vmem_full((coarse_dev, c2)), vmem_full((noct, c2, LANES))],
        out_specs=[vmem_full((keys + SUB, LANES)), vmem_full((vdev, LANES))],
        out_shape=[shape((keys + SUB, LANES), F32), shape((vdev, LANES), F32)],
        compiler_params=params(),
        name="parents",
    )(own_key, grad_coarse.T, down_pad)

    *received, index, w_forward, w_backward, wide, rows = lax.optimization_barrier(
        (*received, index, w_forward, w_backward, wide, rows)
    )
    digits = jnp.stack([got[halo : halo + 2] for got in received]).astype(F32)
    got_keys = (digits[:, 0] * DIGIT + digits[:, 1]).astype(I32).reshape(1, levels * slots)
    answers = pl.pallas_call(
        functools.partial(answer_kernel, levels),
        in_specs=[smem_full((1, levels * slots)), vmem_full((keys + SUB, LANES))],
        out_specs=[vmem_full((slots, LANES))] * levels,
        out_shape=[shape((slots, LANES), BF16)] * levels,
        scratch_shapes=[pltpu.VMEM((levels * slots, LANES), F32)],
        compiler_params=params(),
        name="answer",
    )(got_keys, wide)
    returned = [from_partner(answers[level], level, bits_member) for level in range(levels)]

    stages, width, chunk = 4, 1024, 512
    staging = [pltpu.SMEM((1, width), I32)] * stages
    gathered = pl.pallas_call(
        functools.partial(gather_kernel, levels, halo),
        grid=(kvol,),
        in_specs=[
            pl.BlockSpec(memory_space=pl.ANY),
            vmem_full((vdev, LANES)),
        ]
        + [vmem_full((halo + 2 * SUB, LANES))] * levels,
        out_specs=pl.BlockSpec((vdev, LANES), lambda k: (0, k)),
        out_shape=shape((vdev, kvol * LANES), BF16),
        scratch_shapes=[pltpu.VMEM((table_rows, LANES), F32)]
        + [pltpu.VMEM((chunk, LANES), F32)] * 2
        + staging
        + [pltpu.SemaphoreType.DMA((stages,))],
        compiler_params=params(),
        cost_estimate=pl.CostEstimate(flops=0, bytes_accessed=300_000_000, transcendentals=0),
        name="gather",
    )(index, table, *received)
    pre = jnp.dot(gathered, w_forward, preferred_element_type=F32)

    middle = pl.pallas_call(
        functools.partial(middle_kernel, levels),
        in_specs=[smem_full((1, levels * slots))]
        + [vmem_full((vdev, LANES))] * 2
        + [vmem_full((slots, LANES))] * levels,
        out_specs=[vmem_full((vdev, LANES)), vmem_full((LANES, vdev)), vmem_full((vdev, LANES))]
        + [vmem_full((slots, LANES))] * levels,
        out_shape=[shape((vdev, LANES), BF16), shape((LANES, vdev), BF16), shape((vdev, LANES), F32)]
        + [shape((slots, LANES), BF16)] * levels,
        scratch_shapes=[
            pltpu.VMEM((vdev + SUB, LANES), F32),
            pltpu.VMEM((levels * slots, LANES), F32),
            pltpu.VMEM((vdev + SUB, LANES), F32),
            pltpu.VMEM((levels * slots, LANES), F32),
        ],
        compiler_params=params(),
        name="middle",
    )(send_list, pre, rows, *returned)
    grad_pre, grad_turned, act = middle[:3]
    came = [from_partner(middle[3 + level], level, bits_member) for level in range(levels)]

    group = 3
    grad_w = pl.pallas_call(
        weights_kernel,
        grid=(kvol // group,),
        in_specs=[vmem_full((LANES, vdev)), pl.BlockSpec((vdev, group * LANES), lambda k: (0, k))],
        out_specs=pl.BlockSpec((group * chans, LANES), lambda k: (k, 0)),
        out_shape=shape((kvol * chans, LANES), BF16),
        compiler_params=params(),
        cost_estimate=pl.CostEstimate(flops=0, bytes_accessed=40_000_000, transcendentals=0),
        name="weights",
    )(grad_turned, gathered)

    coarse_out, grad_down = pl.pallas_call(
        functools.partial(pool_kernel, levels, chans),
        in_specs=[
            smem_full((1, levels * slots)),
            smem_full((1, vdev)),
            vmem_full((vdev, LANES)),
            vmem_full((c2, coarse_dev)),
            vmem_full((noct, c2, LANES)),
        ]
        + [vmem_full((slots, LANES))] * levels,
        out_specs=[vmem_full((c2, coarse_dev)), vmem_full((noct * c2 - lane_pad, LANES))],
        out_shape=[shape((c2, coarse_dev), BF16), shape((noct * c2 - lane_pad, LANES), BF16)],
        scratch_shapes=[pltpu.VMEM((levels * slots, LANES), F32)]
        + [pltpu.VMEM((keys + SUB, LANES), F32)] * 8,
        compiler_params=params(),
        name="pool",
    )(got_keys, own_key, act, grad_coarse, down_pad, *came)

    both = ("group", "member")
    devices = lax.axis_size(both)
    packed = jnp.concatenate([grad_w, grad_down], axis=0)
    share = packed.shape[0] // devices
    parts = lax.all_to_all(
        packed.reshape(devices, share, LANES), both, split_axis=0, concat_axis=0, tiled=True
    )
    summed = jnp.sum(parts.astype(F32), axis=0)
    summed, grad_pre = lax.optimization_barrier((summed, grad_pre))
    full = lax.all_gather(summed, both, axis=0, tiled=True)

    accumulators = 8
    scattered = pl.pallas_call(
        functools.partial(scatter_kernel, levels, halo, stages),
        grid=(kvol,),
        in_specs=[
            pl.BlockSpec(memory_space=pl.ANY),
            vmem_full((vdev, LANES)),
            vmem_full((kvol, LANES, LANES)),
        ],
        out_specs=[vmem_full((vdev, LANES))] + [vmem_full((halo, LANES))] * levels,
        out_shape=[shape((vdev, LANES), F32)] + [shape((halo, LANES), BF16)] * levels,
        scratch_shapes=[pltpu.VMEM((chunk, LANES), F32)] * 2
        + staging
        + [pltpu.VMEM((table_rows, LANES), F32)] * accumulators
        + [pltpu.SemaphoreType.DMA((stages,))],
        compiler_params=params(),
        cost_estimate=pl.CostEstimate(flops=0, bytes_accessed=400_000_000, transcendentals=0),
        name="scatter",
    )(index, grad_pre, w_backward)
    incoming = [from_partner(scattered[1 + level], level, bits_member) for level in range(levels)]

    grad_feats = pl.pallas_call(
        functools.partial(finish_kernel, levels),
        in_specs=[smem_full((1, levels * halo)), vmem_full((vdev, LANES))] + [vmem_full((halo, LANES))] * levels,
        out_specs=vmem_full((chans, vdev)),
        out_shape=shape((chans, vdev), F32),
        scratch_shapes=[pltpu.VMEM((levels * halo, LANES), F32)] + [pltpu.VMEM((vdev, LANES), F32)] * 4,
        compiler_params=params(),
        name="finish",
    )(outgoing, scattered[0], *incoming)
    grad_w, grad_down = pl.pallas_call(
        unpack_kernel,
        in_specs=[vmem_full((devices * share, LANES))],
        out_specs=[vmem_full((kvol, chans, chans)), vmem_full((noct, c2, chans))],
        out_shape=[shape((kvol, chans, chans), F32), shape((noct, c2, chans), F32)],
        compiler_params=params(),
        name="unpack",
    )(full)
    return coarse_out, grad_feats, grad_w, grad_down


def solution(mesh):
    both = ("group", "member")
    in_specs = (
        P(None, both),
        P(None, both),
        P(both, None, None),
        P(),
        P(both, None),
        P(both),
        P(both),
        P(),
        P(None, both),
    )
    out_specs = (P(None, both), P(None, both), P(), P())
    return jax.shard_map(shards, mesh=mesh, in_specs=in_specs, out_specs=out_specs, check_vma=False)
```

```python
import functools

import jax
import jax.numpy as jnp
from jax import lax
from jax.experimental import pallas as pl
from jax.experimental.pallas import tpu as pltpu
from jax.sharding import PartitionSpec as P

LANES = 128
SUB = 8
DIGIT = 64
SMEM = pltpu.SMEM
F32 = jnp.float32
BF16 = jnp.bfloat16
I32 = jnp.int32


def from_partner(value, level, bits_member):
    axis, stride = ("member", level) if level < bits_member else ("group", level - bits_member)
    mask = 2**stride
    pairs = [(source, source ^ mask) for source in range(lax.axis_size(axis))]
    return lax.ppermute(value, axis, pairs)


def vmem_full(shape):
    return pl.BlockSpec(shape, lambda *_: (0,) * len(shape))


def smem_full(shape):
    return pl.BlockSpec(shape, lambda *_: (0,) * len(shape), memory_space=SMEM)


def clear(tables):
    count = tables[0].shape[0]
    block = max(b for b in range(SUB, 257, SUB) if count % b == 0)

    def body(step, _):
        part = pl.ds(pl.multiple_of(step * block, block), block)
        for table in tables:
            table[part, :] = jnp.zeros((block, LANES), F32)
        return 0

    lax.fori_loop(0, count // block, body, 0)


def copy_rows(count, unroll, index, source, target):
    def body(step, _):
        base = pl.multiple_of(step * unroll, unroll)
        for j in range(unroll):
            target[pl.ds(base + j, 1), :] = source[pl.ds(index(base + j), 1), :]
        return 0

    lax.fori_loop(0, count // unroll, body, 0)


def add_rows(count, unroll, index, source, tables):
    lanes = len(tables)

    def body(step, _):
        base = pl.multiple_of(step * unroll, unroll)
        for start in range(0, unroll, lanes):
            spots = [index(base + start + j) for j in range(lanes)]
            sums = [
                tables[j][pl.ds(spots[j], 1), :] + source[pl.ds(base + start + j, 1), :]
                for j in range(lanes)
            ]
            for j in range(lanes):
                tables[j][pl.ds(spots[j], 1), :] = sums[j]
        return 0

    lax.fori_loop(0, count // unroll, body, 0)


def prepare_kernel(levels, me_ref, rows_ref, owner_ref, coarse_ref, octant_ref, feats_ref, *refs, noct, coarse_dev, slots):
    messages = refs[:levels]
    table_ref, self_ref, list_ref, pos_ref, buf = refs[levels:]
    chans, vdev = feats_ref.shape
    halo = rows_ref.shape[1] // levels
    noct_keys = noct * coarse_dev
    fill = jnp.zeros((LANES - chans, LANES), F32)
    for c in range(vdev // LANES):
        cols = pl.ds(c * LANES, LANES)
        block = jnp.concatenate([feats_ref[:, cols].astype(F32), fill], axis=0)
        table_ref[cols, :] = block.T
    copy_rows(levels * halo, 64, lambda r: rows_ref[0, r], table_ref, buf)

    differ = jnp.bitwise_xor(owner_ref[...], me_ref[0])
    level_id = lax.broadcasted_iota(I32, (SUB, LANES), 0)
    bit = jnp.where(level_id < levels, jnp.left_shift(jnp.ones_like(level_id), level_id), 0)
    chunks = vdev // LANES
    classes = []
    for c in range(chunks):
        part = jnp.broadcast_to(differ[:, c * LANES : (c + 1) * LANES], (SUB, LANES))
        classes.append(jnp.where((part == bit) & (level_id < levels), 1.0, 0.0).astype(F32))
    upper = lax.broadcasted_iota(I32, (LANES, LANES), 0) <= lax.broadcasted_iota(I32, (LANES, LANES), 1)
    prefix = jnp.dot(
        jnp.concatenate(classes, axis=0).astype(BF16),
        jnp.where(upper, 1.0, 0.0).astype(BF16),
        preferred_element_type=F32,
    )
    carry = jnp.zeros((SUB, 1), F32)
    start = (level_id * slots).astype(F32)
    digit_rows = []
    digit_id = lax.broadcasted_iota(I32, (SUB, LANES), 0)
    for c in range(chunks):
        cols = pl.ds(c * LANES, LANES)
        inclusive = prefix[c * SUB : (c + 1) * SUB]
        spot = classes[c] * (start + inclusive - 1.0 + carry)
        carry = carry + inclusive[:, LANES - 1 :]
        remote = jnp.sum(classes[c], axis=0, keepdims=True) > 0.5
        position = jnp.where(remote, jnp.sum(spot, axis=0, keepdims=True).astype(I32), levels * slots)
        keys = octant_ref[:, cols] * coarse_dev + coarse_ref[:, cols]
        pos_ref[:, cols] = position
        self_ref[:, cols] = jnp.where(remote, noct_keys, keys)
        voxel = lax.broadcasted_iota(I32, (SUB, LANES), 1) + c * LANES
        number = jnp.where(digit_id < 2, jnp.broadcast_to(keys, (SUB, LANES)), voxel)
        high = lax.shift_right_logical(number, 6) - DIGIT
        low = number & (DIGIT - 1)
        digits = jnp.where(digit_id < 4, jnp.where((digit_id & 1) == 0, high, low), 0)
        digit_rows.append(digits.astype(F32).astype(BF16))
    digits = jnp.concatenate(digit_rows, axis=1)
    slot_id = lax.broadcasted_iota(I32, (slots, LANES), 0)
    for level in range(levels):
        hot = []
        for c in range(chunks):
            position = jnp.broadcast_to(pos_ref[:, pl.ds(c * LANES, LANES)], (slots, LANES))
            hot.append(jnp.where(position == slot_id + level * slots, 1.0, 0.0).astype(BF16))
        found = lax.dot_general(
            digits, jnp.concatenate(hot, axis=1), (((1,), (1,)), ((), ())), preferred_element_type=F32
        )
        found = found + jnp.where((digit_id & 1) == 0, float(DIGIT), 0.0)
        list_ref[:, pl.ds(level * slots, slots)] = (found[2:3] * float(DIGIT) + found[3:4]).astype(I32)
        messages[level][pl.ds(0, halo), :] = buf[pl.ds(level * halo, halo), :].astype(BF16)
        messages[level][pl.ds(halo, 2 * SUB), :] = jnp.concatenate(
            [found, jnp.zeros((SUB, LANES), F32)], axis=0
        ).astype(BF16)


def parents_kernel(self_ref, coarse_ref, weight_ref, wide_ref, rows_ref):
    noct = weight_ref.shape[0]
    ndev = coarse_ref.shape[0]
    for o in range(noct):
        grad = jnp.dot(coarse_ref[...], weight_ref[o], preferred_element_type=F32)
        wide_ref[pl.ds(o * ndev, ndev), :] = grad.astype(BF16).astype(F32)
    wide_ref[pl.ds(noct * ndev, SUB), :] = jnp.zeros((SUB, LANES), F32)
    copy_rows(rows_ref.shape[0], 64, lambda r: self_ref[0, r], wide_ref, rows_ref)


def answer_kernel(levels, keys_ref, wide_ref, *refs):
    outs = refs[:levels]
    buf = refs[levels]
    slots = outs[0].shape[0]
    copy_rows(levels * slots, 64, lambda r: keys_ref[0, r], wide_ref, buf)
    for level in range(levels):
        outs[level][...] = buf[pl.ds(level * slots, slots), :].astype(BF16)


def index_copy(index_ref, piece, store, sem, width):
    pieces = index_ref.shape[2] // width
    row = lax.div(piece, pieces)
    start = pl.multiple_of(lax.rem(piece, pieces) * width, width)
    return pltpu.make_async_copy(index_ref.at[row, :, pl.ds(start, width)], store, sem)


def walk(index_ref, stores, sems, vdev, chunk, total, step_of):
    k = pl.program_id(0)
    width = stores[0].shape[1]
    many = len(stores)
    pieces = vdev // width

    @pl.when(k == 0)
    def _():
        for b in range(many):
            index_copy(index_ref, b, stores[b], sems.at[b], width).start()

    def body(turn, _):
        for b in range(many):
            piece = k * pieces + turn * many + b
            index_copy(index_ref, piece, stores[b], sems.at[b], width).wait()
            for sub in range(width // chunk):
                base = pl.multiple_of((turn * many + b) * width + sub * chunk, chunk)
                step_of(base, (b * (width // chunk) + sub) % 2, stores[b], sub * chunk)

            @pl.when(piece + many < total * pieces)
            def _():
                index_copy(index_ref, piece + many, stores[b], sems.at[b], width).start()

        return 0

    lax.fori_loop(0, pieces // many, body, 0)


def gather_kernel(levels, halo, index_ref, local_ref, *refs):
    received = refs[:levels]
    out_ref, table, buf0, buf1 = refs[levels : levels + 4]
    stores = refs[levels + 4 : -1]
    sems = refs[-1]
    bufs = (buf0, buf1)
    vdev = local_ref.shape[0]
    chunk = buf0.shape[0]

    @pl.when(pl.program_id(0) == 0)
    def _():
        table[pl.ds(0, vdev), :] = local_ref[...]
        for level in range(levels):
            table[pl.ds(vdev + level * halo, halo), :] = received[level][pl.ds(0, halo), :].astype(F32)
        table[pl.ds(vdev + levels * halo, SUB), :] = jnp.zeros((SUB, LANES), F32)
        buf1[...] = jnp.zeros_like(buf1)

    last = pl.num_programs(0) - 1

    def step(base, parity, store, entry):
        buf = bufs[parity]
        for j in range(chunk):
            buf[pl.ds(j, 1), :] = table[pl.ds(store[0, entry + j], 1), :]
        behind = pl.multiple_of(jnp.maximum(base - chunk, 0), chunk)
        out_ref[pl.ds(behind, chunk), :] = bufs[1 - parity][...].astype(BF16)

    @pl.when(pl.program_id(0) < last)
    def _():
        walk(index_ref, stores, sems, vdev, chunk, last, step)
        out_ref[pl.ds(vdev - chunk, chunk), :] = buf1[...].astype(BF16)

    @pl.when(pl.program_id(0) == last)
    def _():
        out_ref[...] = local_ref[...].astype(BF16)


def middle_kernel(levels, list_ref, pre_ref, rows_ref, *refs):
    returned = refs[:levels]
    grad_ref, turned_ref, act_ref = refs[levels : levels + 3]
    sends = refs[levels + 3 : 2 * levels + 3]
    rows, back, act, out = refs[2 * levels + 3 :]
    vdev = pre_ref.shape[0]
    slots = returned[0].shape[0]
    rows[pl.ds(0, vdev), :] = rows_ref[...]
    for level in range(levels):
        back[pl.ds(level * slots, slots), :] = returned[level][...].astype(F32)

    def patch(step, _):
        base = pl.multiple_of(step * 64, 64)
        for j in range(64):
            rows[pl.ds(list_ref[0, base + j], 1), :] = back[pl.ds(base + j, 1), :]
        return 0

    lax.fori_loop(0, levels * slots // 64, patch, 0)

    def point(step, _):
        part = pl.ds(pl.multiple_of(step * 4 * LANES, 4 * LANES), 4 * LANES)
        pre = pre_ref[part, :]
        sig = 1.0 / (1.0 + jnp.exp(-pre))
        value = (pre * sig).astype(BF16).astype(F32)
        act[part, :] = value
        act_ref[part, :] = value
        grad = rows[part, :] * (sig * (1.0 + pre * (1.0 - sig)))
        grad_ref[part, :] = grad.astype(BF16)
        turned_ref[:, part] = grad.T.astype(BF16)
        return 0

    lax.fori_loop(0, vdev // (4 * LANES), point, 0)
    act[pl.ds(vdev, SUB), :] = jnp.zeros((SUB, LANES), F32)
    copy_rows(levels * slots, 64, lambda r: list_ref[0, r], act, out)
    for level in range(levels):
        sends[level][...] = out[pl.ds(level * slots, slots), :].astype(BF16)


def weights_kernel(turned_ref, taken_ref, out_ref):
    wide = jnp.dot(turned_ref[...], taken_ref[...], preferred_element_type=F32)
    many = wide.shape[1] // LANES
    rows = out_ref.shape[0] // many
    for j in range(many):
        out_ref[pl.ds(j * rows, rows), :] = wide[:rows, j * LANES : (j + 1) * LANES].astype(BF16)


def unpack_kernel(full_ref, weights_ref, down_ref):
    kvol, chans, _ = weights_ref.shape
    noct, c2, _ = down_ref.shape
    centre = kvol // 2
    for k in range(kvol):
        spot = kvol - 1 if k == centre else k - int(k > centre)
        weights_ref[k] = full_ref[pl.ds(spot * chans, chans), :][:, :chans]
    first = kvol * chans
    rest = LANES - chans
    for o in range(noct - 1):
        down_ref[o] = full_ref[pl.ds(first + o * c2, c2), :][:, :chans]
    start = first + (noct - 1) * c2
    down_ref[noct - 1, pl.ds(0, c2 - rest), :] = full_ref[pl.ds(start, c2 - rest), :][:, :chans]
    lane = lax.broadcasted_iota(I32, (rest, LANES), 1)
    tail = jnp.zeros((rest, LANES), F32)
    for j in range(chans // rest):
        piece = pltpu.roll(full_ref[pl.ds(first + j * rest, rest), :], rest * (j + 1), 1)
        tail = jnp.where((lane >= j * rest) & (lane < (j + 1) * rest), piece, tail)
    down_ref[noct - 1, pl.ds(c2 - rest, rest), :] = tail[:, :chans]


def pool_kernel(levels, chans, keys_ref, self_ref, act_ref, grad_ref, weight_ref, *refs):
    received = refs[:levels]
    coarse_ref, down_ref, rows = refs[levels : levels + 3]
    pools = refs[levels + 3 :]
    slots = received[0].shape[0]
    noct, c2, _ = weight_ref.shape
    rest = LANES - chans
    ndev = grad_ref.shape[1]
    for level in range(levels):
        rows[pl.ds(level * slots, slots), :] = received[level][...].astype(F32)
    clear(pools)
    add_rows(act_ref.shape[0], 64, lambda r: self_ref[0, r], act_ref, pools)
    add_rows(levels * slots, 64, lambda r: keys_ref[0, r], rows, pools)
    coarse = jnp.zeros(coarse_ref.shape, F32)
    lane = lax.broadcasted_iota(I32, (rest, LANES), 1)
    for o in reversed(range(noct)):
        part = pl.ds(o * ndev, ndev)
        total = pools[0][part, :]
        for pool in pools[1:]:
            total = total + pool[part, :]
        pooled = total.astype(BF16)
        coarse = coarse + lax.dot_general(
            weight_ref[o], pooled, (((1,), (1,)), ((), ())), preferred_element_type=F32
        )
        down = jnp.dot(grad_ref[...], pooled, preferred_element_type=F32)
        if o == noct - 1:
            tail = down[c2 - rest :]
            down = down[: c2 - rest]
        if o == 0:
            parts = []
            for j in range(chans // rest):
                piece = pltpu.roll(tail, (chans - rest * j) % LANES, 1)
                parts.append(jnp.where(lane >= chans, piece, down[j * rest : (j + 1) * rest]))
            down = jnp.concatenate(parts + [down[chans:]], axis=0)
        down_ref[pl.ds(o * c2, down.shape[0]), :] = down.astype(BF16)
    coarse_ref[...] = coarse.astype(BF16)


def scatter_kernel(levels, halo, stages, index_ref, grad_ref, weight_ref, local_ref, *refs):
    backs = refs[:levels]
    buf0, buf1 = refs[levels : levels + 2]
    stores = refs[levels + 2 : levels + 2 + stages]
    tables = refs[levels + 2 + stages : -1]
    sems = refs[-1]
    bufs = (buf0, buf1)
    vdev = local_ref.shape[0]
    chunk = buf0.shape[0]
    lanes = len(tables)
    k = pl.program_id(0)
    last = pl.num_programs(0) - 1

    def ready(base, offset, buf):
        buf[...] = jnp.dot(grad_ref[pl.ds(base, chunk), :], weight_ref[offset], preferred_element_type=F32)

    @pl.when(k == 0)
    def _():
        clear(tables)
        ready(0, 0, buf0)

    def step(base, parity, store, entry):
        buf = bufs[parity]
        over = base + chunk == vdev
        ahead = pl.multiple_of(jnp.where(over, 0, base + chunk), chunk)
        ready(ahead, jnp.minimum(jnp.where(over, k + 1, k), last), bufs[1 - parity])
        for start in range(0, chunk, lanes):
            now = min(lanes, chunk - start)
            spots = [store[0, entry + start + j] for j in range(now)]
            sums = [tables[j][pl.ds(spots[j], 1), :] + buf[pl.ds(start + j, 1), :] for j in range(now)]
            for j in range(now):
                tables[j][pl.ds(spots[j], 1), :] = sums[j]

    walk(index_ref, stores, sems, vdev, chunk, last + 1, step)

    @pl.when(k == last)
    def _():
        def total(part):
            result = tables[0][part, :]
            for table in tables[1:]:
                result = result + table[part, :]
            return result

        def close(step, _):
            part = pl.ds(pl.multiple_of(step * chunk, chunk), chunk)
            centre = jnp.dot(grad_ref[part, :], weight_ref[last + 1], preferred_element_type=F32)
            local_ref[part, :] = total(part) + centre
            return 0

        lax.fori_loop(0, vdev // chunk, close, 0)
        for level in range(levels):
            backs[level][...] = total(pl.ds(vdev + level * halo, halo)).astype(BF16)


def finish_kernel(levels, rows_ref, local_ref, *refs):
    incoming = refs[:levels]
    out_ref, rows = refs[levels : levels + 2]
    tables = refs[levels + 2 :]
    halo = incoming[0].shape[0]
    chans, vdev = out_ref.shape
    for level in range(levels):
        rows[pl.ds(level * halo, halo), :] = incoming[level][...].astype(F32)
    clear(tables)
    add_rows(levels * halo, 64, lambda r: rows_ref[0, r], rows, tables)

    def close(step, _):
        part = pl.ds(pl.multiple_of(step * 2 * LANES, 2 * LANES), 2 * LANES)
        total = local_ref[part, :]
        for table in tables:
            total = total + table[part, :]
        out_ref[:, part] = total.T[:chans]
        return 0

    lax.fori_loop(0, vdev // (2 * LANES), close, 0)


def shape(dims, dtype):
    return jax.ShapeDtypeStruct(dims, dtype)


def params():
    return pltpu.CompilerParams(vmem_limit_bytes=56 << 20)


def shards(feats, kmap, send_rows, w_sub, owner, coarse_id, octant, w_down, grad_coarse):
    chans, vdev = feats.shape
    _, levels, halo = send_rows.shape
    kvol = kmap.shape[0]
    noct, c2, _ = w_down.shape
    coarse_dev = grad_coarse.shape[1]
    keys = noct * coarse_dev
    slots = vdev // 32
    bits_member = lax.axis_size("member").bit_length() - 1
    myself = lax.axis_index(("group", "member")).astype(I32).reshape(1)
    lane_pad = LANES - chans
    outgoing = send_rows.reshape(1, levels * halo)
    table_rows = vdev + levels * halo + SUB
    middle_k = kvol // 2
    index = jnp.concatenate([kmap[:middle_k], kmap[middle_k + 1 :]], axis=0).reshape(kvol - 1, 1, vdev)

    w_ordered = jnp.concatenate([w_sub[:middle_k], w_sub[middle_k + 1 :], w_sub[middle_k : middle_k + 1]], axis=0)
    w_backward = jnp.pad(w_ordered, ((0, 0), (0, lane_pad), (0, lane_pad)))
    w_forward = w_backward.transpose(0, 2, 1).reshape(kvol * LANES, LANES)
    down_pad = jnp.pad(w_down, ((0, 0), (0, 0), (0, lane_pad)))

    prepared = pl.pallas_call(
        functools.partial(prepare_kernel, levels, noct=noct, coarse_dev=coarse_dev, slots=slots),
        in_specs=[pl.BlockSpec(memory_space=SMEM), smem_full((1, levels * halo))]
        + [vmem_full((1, vdev))] * 3
        + [vmem_full((chans, vdev))],
        out_specs=[vmem_full((halo + 2 * SUB, LANES))] * levels
        + [vmem_full((vdev, LANES)), vmem_full((1, vdev)), vmem_full((1, levels * slots))],
        out_shape=[shape((halo + 2 * SUB, LANES), BF16)] * levels
        + [shape((vdev, LANES), F32), shape((1, vdev), I32), shape((1, levels * slots), I32)],
        scratch_shapes=[pltpu.VMEM((1, vdev), I32), pltpu.VMEM((levels * halo, LANES), F32)],
        compiler_params=params(),
        name="prepare",
    )(myself, outgoing, owner.reshape(1, vdev), coarse_id.reshape(1, vdev), octant.reshape(1, vdev), feats)
    messages = prepared[:levels]
    table, own_key, send_list = prepared[levels:]
    received = [from_partner(messages[level], level, bits_member) for level in range(levels)]

    wide, rows = pl.pallas_call(
        parents_kernel,
        in_specs=[smem_full((1, vdev)), vmem_full((coarse_dev, c2)), vmem_full((noct, c2, LANES))],
        out_specs=[vmem_full((keys + SUB, LANES)), vmem_full((vdev, LANES))],
        out_shape=[shape((keys + SUB, LANES), F32), shape((vdev, LANES), F32)],
        compiler_params=params(),
        name="parents",
    )(own_key, grad_coarse.T, down_pad)

    *received, index, w_forward, w_backward, wide, rows = lax.optimization_barrier(
        (*received, index, w_forward, w_backward, wide, rows)
    )
    digits = jnp.stack([got[halo : halo + 2] for got in received]).astype(F32)
    got_keys = (digits[:, 0] * DIGIT + digits[:, 1]).astype(I32).reshape(1, levels * slots)
    answers = pl.pallas_call(
        functools.partial(answer_kernel, levels),
        in_specs=[smem_full((1, levels * slots)), vmem_full((keys + SUB, LANES))],
        out_specs=[vmem_full((slots, LANES))] * levels,
        out_shape=[shape((slots, LANES), BF16)] * levels,
        scratch_shapes=[pltpu.VMEM((levels * slots, LANES), F32)],
        compiler_params=params(),
        name="answer",
    )(got_keys, wide)
    returned = [from_partner(answers[level], level, bits_member) for level in range(levels)]

    stages, width, chunk = 4, 1024, 512
    staging = [pltpu.SMEM((1, width), I32)] * stages
    gathered = pl.pallas_call(
        functools.partial(gather_kernel, levels, halo),
        grid=(kvol,),
        in_specs=[
            pl.BlockSpec(memory_space=pl.ANY),
            vmem_full((vdev, LANES)),
        ]
        + [vmem_full((halo + 2 * SUB, LANES))] * levels,
        out_specs=pl.BlockSpec((vdev, LANES), lambda k: (0, k)),
        out_shape=shape((vdev, kvol * LANES), BF16),
        scratch_shapes=[pltpu.VMEM((table_rows, LANES), F32)]
        + [pltpu.VMEM((chunk, LANES), F32)] * 2
        + staging
        + [pltpu.SemaphoreType.DMA((stages,))],
        compiler_params=params(),
        cost_estimate=pl.CostEstimate(flops=0, bytes_accessed=300_000_000, transcendentals=0),
        name="gather",
    )(index, table, *received)
    pre = jnp.dot(gathered, w_forward, preferred_element_type=F32)

    middle = pl.pallas_call(
        functools.partial(middle_kernel, levels),
        in_specs=[smem_full((1, levels * slots))]
        + [vmem_full((vdev, LANES))] * 2
        + [vmem_full((slots, LANES))] * levels,
        out_specs=[vmem_full((vdev, LANES)), vmem_full((LANES, vdev)), vmem_full((vdev, LANES))]
        + [vmem_full((slots, LANES))] * levels,
        out_shape=[shape((vdev, LANES), BF16), shape((LANES, vdev), BF16), shape((vdev, LANES), F32)]
        + [shape((slots, LANES), BF16)] * levels,
        scratch_shapes=[
            pltpu.VMEM((vdev + SUB, LANES), F32),
            pltpu.VMEM((levels * slots, LANES), F32),
            pltpu.VMEM((vdev + SUB, LANES), F32),
            pltpu.VMEM((levels * slots, LANES), F32),
        ],
        compiler_params=params(),
        name="middle",
    )(send_list, pre, rows, *returned)
    grad_pre, grad_turned, act = middle[:3]
    came = [from_partner(middle[3 + level], level, bits_member) for level in range(levels)]

    group = 3
    grad_w = pl.pallas_call(
        weights_kernel,
        grid=(kvol // group,),
        in_specs=[vmem_full((LANES, vdev)), pl.BlockSpec((vdev, group * LANES), lambda k: (0, k))],
        out_specs=pl.BlockSpec((group * chans, LANES), lambda k: (k, 0)),
        out_shape=shape((kvol * chans, LANES), BF16),
        compiler_params=params(),
        cost_estimate=pl.CostEstimate(flops=0, bytes_accessed=40_000_000, transcendentals=0),
        name="weights",
    )(grad_turned, gathered)

    coarse_out, grad_down = pl.pallas_call(
        functools.partial(pool_kernel, levels, chans),
        in_specs=[
            smem_full((1, levels * slots)),
            smem_full((1, vdev)),
            vmem_full((vdev, LANES)),
            vmem_full((c2, coarse_dev)),
            vmem_full((noct, c2, LANES)),
        ]
        + [vmem_full((slots, LANES))] * levels,
        out_specs=[vmem_full((c2, coarse_dev)), vmem_full((noct * c2 - lane_pad, LANES))],
        out_shape=[shape((c2, coarse_dev), BF16), shape((noct * c2 - lane_pad, LANES), BF16)],
        scratch_shapes=[pltpu.VMEM((levels * slots, LANES), F32)]
        + [pltpu.VMEM((keys + SUB, LANES), F32)] * 8,
        compiler_params=params(),
        name="pool",
    )(got_keys, own_key, act, grad_coarse, down_pad, *came)

    both = ("group", "member")
    devices = lax.axis_size(both)
    packed = jnp.concatenate([grad_w, grad_down], axis=0)
    share = packed.shape[0] // devices
    parts = lax.all_to_all(
        packed.reshape(devices, share, LANES), both, split_axis=0, concat_axis=0, tiled=True
    )
    summed = jnp.sum(parts.astype(F32), axis=0)
    summed, grad_pre = lax.optimization_barrier((summed, grad_pre))
    full = lax.all_gather(summed, both, axis=0, tiled=True)

    accumulators = 8
    scattered = pl.pallas_call(
        functools.partial(scatter_kernel, levels, halo, stages),
        grid=(kvol - 1,),
        in_specs=[
            pl.BlockSpec(memory_space=pl.ANY),
            vmem_full((vdev, LANES)),
            vmem_full((kvol, LANES, LANES)),
        ],
        out_specs=[vmem_full((vdev, LANES))] + [vmem_full((halo, LANES))] * levels,
        out_shape=[shape((vdev, LANES), F32)] + [shape((halo, LANES), BF16)] * levels,
        scratch_shapes=[pltpu.VMEM((chunk, LANES), F32)] * 2
        + staging
        + [pltpu.VMEM((table_rows, LANES), F32)] * accumulators
        + [pltpu.SemaphoreType.DMA((stages,))],
        compiler_params=params(),
        cost_estimate=pl.CostEstimate(flops=0, bytes_accessed=400_000_000, transcendentals=0),
        name="scatter",
    )(index, grad_pre, w_backward)
    incoming = [from_partner(scattered[1 + level], level, bits_member) for level in range(levels)]

    grad_w, grad_down = pl.pallas_call(
        unpack_kernel,
        in_specs=[vmem_full((devices * share, LANES))],
        out_specs=[vmem_full((kvol, chans, chans)), vmem_full((noct, c2, chans))],
        out_shape=[shape((kvol, chans, chans), F32), shape((noct, c2, chans), F32)],
        compiler_params=params(),
        name="unpack",
    )(full)
    *incoming, grad_w, grad_down = lax.optimization_barrier((*incoming, grad_w, grad_down))

    grad_feats = pl.pallas_call(
        functools.partial(finish_kernel, levels),
        in_specs=[smem_full((1, levels * halo)), vmem_full((vdev, LANES))] + [vmem_full((halo, LANES))] * levels,
        out_specs=vmem_full((chans, vdev)),
        out_shape=shape((chans, vdev), F32),
        scratch_shapes=[pltpu.VMEM((levels * halo, LANES), F32)] + [pltpu.VMEM((vdev, LANES), F32)] * 8,
        compiler_params=params(),
        name="finish",
    )(outgoing, scattered[0], *incoming)
    return coarse_out, grad_feats, grad_w, grad_down


def solution(mesh):
    both = ("group", "member")
    in_specs = (
        P(None, both),
        P(None, both),
        P(both, None, None),
        P(),
        P(both, None),
        P(both),
        P(both),
        P(),
        P(None, both),
    )
    out_specs = (P(None, both), P(None, both), P(), P())
    return jax.shard_map(shards, mesh=mesh, in_specs=in_specs, out_specs=out_specs, check_vma=False)
```

```python
import functools

import jax
import jax.numpy as jnp
from jax import lax
from jax.experimental import pallas as pl
from jax.experimental.pallas import tpu as pltpu
from jax.sharding import PartitionSpec as P

LANES = 128
SUB = 8
DIGIT = 64
SMEM = pltpu.SMEM
F32 = jnp.float32
BF16 = jnp.bfloat16
I32 = jnp.int32


def from_partner(value, level, bits_member):
    axis, stride = ("member", level) if level < bits_member else ("group", level - bits_member)
    mask = 2**stride
    pairs = [(source, source ^ mask) for source in range(lax.axis_size(axis))]
    return lax.ppermute(value, axis, pairs)


def vmem_full(shape):
    return pl.BlockSpec(shape, lambda *_: (0,) * len(shape))


def smem_full(shape):
    return pl.BlockSpec(shape, lambda *_: (0,) * len(shape), memory_space=SMEM)


def clear(tables):
    count = tables[0].shape[0]
    block = max(b for b in range(SUB, 257, SUB) if count % b == 0)

    def body(step, _):
        part = pl.ds(pl.multiple_of(step * block, block), block)
        for table in tables:
            table[part, :] = jnp.zeros((block, LANES), F32)
        return 0

    lax.fori_loop(0, count // block, body, 0)


def copy_rows(count, unroll, index, source, target):
    def body(step, _):
        base = pl.multiple_of(step * unroll, unroll)
        for j in range(unroll):
            target[pl.ds(base + j, 1), :] = source[pl.ds(index(base + j), 1), :]
        return 0

    lax.fori_loop(0, count // unroll, body, 0)


def add_rows(count, unroll, index, source, tables):
    lanes = len(tables)

    def body(step, _):
        base = pl.multiple_of(step * unroll, unroll)
        for start in range(0, unroll, lanes):
            spots = [index(base + start + j) for j in range(lanes)]
            sums = [
                tables[j][pl.ds(spots[j], 1), :] + source[pl.ds(base + start + j, 1), :]
                for j in range(lanes)
            ]
            for j in range(lanes):
                tables[j][pl.ds(spots[j], 1), :] = sums[j]
        return 0

    lax.fori_loop(0, count // unroll, body, 0)


def prepare_kernel(levels, me_ref, rows_ref, owner_ref, coarse_ref, octant_ref, feats_ref, *refs, noct, coarse_dev, slots):
    messages = refs[:levels]
    table_ref, self_ref, list_ref, pos_ref, buf = refs[levels:]
    chans, vdev = feats_ref.shape
    halo = rows_ref.shape[1] // levels
    noct_keys = noct * coarse_dev
    fill = jnp.zeros((LANES - chans, LANES), F32)
    for c in range(vdev // LANES):
        cols = pl.ds(c * LANES, LANES)
        block = jnp.concatenate([feats_ref[:, cols].astype(F32), fill], axis=0)
        table_ref[cols, :] = block.T
    copy_rows(levels * halo, 64, lambda r: rows_ref[0, r], table_ref, buf)

    differ = jnp.bitwise_xor(owner_ref[...], me_ref[0])
    level_id = lax.broadcasted_iota(I32, (SUB, LANES), 0)
    bit = jnp.where(level_id < levels, jnp.left_shift(jnp.ones_like(level_id), level_id), 0)
    chunks = vdev // LANES
    classes = []
    for c in range(chunks):
        part = jnp.broadcast_to(differ[:, c * LANES : (c + 1) * LANES], (SUB, LANES))
        classes.append(jnp.where((part == bit) & (level_id < levels), 1.0, 0.0).astype(F32))
    upper = lax.broadcasted_iota(I32, (LANES, LANES), 0) <= lax.broadcasted_iota(I32, (LANES, LANES), 1)
    prefix = jnp.dot(
        jnp.concatenate(classes, axis=0).astype(BF16),
        jnp.where(upper, 1.0, 0.0).astype(BF16),
        preferred_element_type=F32,
    )
    carry = jnp.zeros((SUB, 1), F32)
    start = (level_id * slots).astype(F32)
    digit_rows = []
    digit_id = lax.broadcasted_iota(I32, (SUB, LANES), 0)
    for c in range(chunks):
        cols = pl.ds(c * LANES, LANES)
        inclusive = prefix[c * SUB : (c + 1) * SUB]
        spot = classes[c] * (start + inclusive - 1.0 + carry)
        carry = carry + inclusive[:, LANES - 1 :]
        remote = jnp.sum(classes[c], axis=0, keepdims=True) > 0.5
        position = jnp.where(remote, jnp.sum(spot, axis=0, keepdims=True).astype(I32), levels * slots)
        keys = octant_ref[:, cols] * coarse_dev + coarse_ref[:, cols]
        pos_ref[:, cols] = position
        self_ref[:, cols] = jnp.where(remote, noct_keys, keys)
        voxel = lax.broadcasted_iota(I32, (SUB, LANES), 1) + c * LANES
        number = jnp.where(digit_id < 2, jnp.broadcast_to(keys, (SUB, LANES)), voxel)
        high = lax.shift_right_logical(number, 6) - DIGIT
        low = number & (DIGIT - 1)
        digits = jnp.where(digit_id < 4, jnp.where((digit_id & 1) == 0, high, low), 0)
        digit_rows.append(digits.astype(F32).astype(BF16))
    digits = jnp.concatenate(digit_rows, axis=1)
    slot_id = lax.broadcasted_iota(I32, (slots, LANES), 0)
    for level in range(levels):
        hot = []
        for c in range(chunks):
            position = jnp.broadcast_to(pos_ref[:, pl.ds(c * LANES, LANES)], (slots, LANES))
            hot.append(jnp.where(position == slot_id + level * slots, 1.0, 0.0).astype(BF16))
        found = lax.dot_general(
            digits, jnp.concatenate(hot, axis=1), (((1,), (1,)), ((), ())), preferred_element_type=F32
        )
        found = found + jnp.where((digit_id & 1) == 0, float(DIGIT), 0.0)
        list_ref[:, pl.ds(level * slots, slots)] = (found[2:3] * float(DIGIT) + found[3:4]).astype(I32)
        messages[level][pl.ds(0, halo), :] = buf[pl.ds(level * halo, halo), :].astype(BF16)
        messages[level][pl.ds(halo, 2 * SUB), :] = jnp.concatenate(
            [found, jnp.zeros((SUB, LANES), F32)], axis=0
        ).astype(BF16)


def parents_kernel(self_ref, coarse_ref, weight_ref, wide_ref, rows_ref):
    noct = weight_ref.shape[0]
    ndev = coarse_ref.shape[0]
    for o in range(noct):
        grad = jnp.dot(coarse_ref[...], weight_ref[o], preferred_element_type=F32)
        wide_ref[pl.ds(o * ndev, ndev), :] = grad.astype(BF16).astype(F32)
    wide_ref[pl.ds(noct * ndev, SUB), :] = jnp.zeros((SUB, LANES), F32)
    copy_rows(rows_ref.shape[0], 64, lambda r: self_ref[0, r], wide_ref, rows_ref)


def answer_kernel(levels, keys_ref, wide_ref, *refs):
    outs = refs[:levels]
    buf = refs[levels]
    slots = outs[0].shape[0]
    copy_rows(levels * slots, 64, lambda r: keys_ref[0, r], wide_ref, buf)
    for level in range(levels):
        outs[level][...] = buf[pl.ds(level * slots, slots), :].astype(BF16)


def index_copy(index_ref, piece, store, sem, width):
    pieces = index_ref.shape[2] // width
    row = lax.div(piece, pieces)
    start = pl.multiple_of(lax.rem(piece, pieces) * width, width)
    return pltpu.make_async_copy(index_ref.at[row, :, pl.ds(start, width)], store, sem)


def walk(index_ref, stores, sems, vdev, chunk, total, step_of):
    k = pl.program_id(0)
    width = stores[0].shape[1]
    many = len(stores)
    pieces = vdev // width

    @pl.when(k == 0)
    def _():
        for b in range(many):
            index_copy(index_ref, b, stores[b], sems.at[b], width).start()

    def body(turn, _):
        for b in range(many):
            piece = k * pieces + turn * many + b
            index_copy(index_ref, piece, stores[b], sems.at[b], width).wait()
            for sub in range(width // chunk):
                base = pl.multiple_of((turn * many + b) * width + sub * chunk, chunk)
                step_of(base, (b * (width // chunk) + sub) % 2, stores[b], sub * chunk)

            @pl.when(piece + many < total * pieces)
            def _():
                index_copy(index_ref, piece + many, stores[b], sems.at[b], width).start()

        return 0

    lax.fori_loop(0, pieces // many, body, 0)


def gather_kernel(levels, halo, index_ref, local_ref, *refs):
    received = refs[:levels]
    out_ref, table, buf0, buf1 = refs[levels : levels + 4]
    stores = refs[levels + 4 : -1]
    sems = refs[-1]
    bufs = (buf0, buf1)
    vdev = local_ref.shape[0]
    chunk = buf0.shape[0]

    @pl.when(pl.program_id(0) == 0)
    def _():
        table[pl.ds(0, vdev), :] = local_ref[...]
        for level in range(levels):
            table[pl.ds(vdev + level * halo, halo), :] = received[level][pl.ds(0, halo), :].astype(F32)
        table[pl.ds(vdev + levels * halo, SUB), :] = jnp.zeros((SUB, LANES), F32)
        buf1[...] = jnp.zeros_like(buf1)

    last = pl.num_programs(0) - 1

    def step(base, parity, store, entry):
        buf = bufs[parity]
        for j in range(chunk):
            buf[pl.ds(j, 1), :] = table[pl.ds(store[0, entry + j], 1), :]
        behind = pl.multiple_of(jnp.maximum(base - chunk, 0), chunk)
        out_ref[pl.ds(behind, chunk), :] = bufs[1 - parity][...].astype(BF16)

    @pl.when(pl.program_id(0) < last)
    def _():
        walk(index_ref, stores, sems, vdev, chunk, last, step)
        out_ref[pl.ds(vdev - chunk, chunk), :] = buf1[...].astype(BF16)

    @pl.when(pl.program_id(0) == last)
    def _():
        out_ref[...] = local_ref[...].astype(BF16)


def middle_kernel(levels, list_ref, taken_ref, weight_ref, rows_ref, *refs):
    returned = refs[:levels]
    grad_ref, turned_ref, act_ref = refs[levels : levels + 3]
    sends = refs[levels + 3 : 2 * levels + 3]
    rows, back, act, out, pre_buf = refs[2 * levels + 3 :]
    vdev = rows_ref.shape[0]
    slots = returned[0].shape[0]
    block = taken_ref.shape[0]
    piece = 2 * LANES
    turn = pl.program_id(0)

    @pl.when(turn == 0)
    def _():
        rows[pl.ds(0, vdev), :] = rows_ref[...]
        for level in range(levels):
            back[pl.ds(level * slots, slots), :] = returned[level][...].astype(F32)

        def patch(step, _):
            base = pl.multiple_of(step * 64, 64)
            for j in range(64):
                rows[pl.ds(list_ref[0, base + j], 1), :] = back[pl.ds(base + j, 1), :]
            return 0

        lax.fori_loop(0, levels * slots // 64, patch, 0)
        act[pl.ds(vdev, SUB), :] = jnp.zeros((SUB, LANES), F32)

    pre_buf[...] = jnp.dot(taken_ref[...], weight_ref[...], preferred_element_type=F32)

    def point(step, _):
        part = pl.ds(pl.multiple_of(turn * block + step * piece, piece), piece)
        pre = pre_buf[pl.ds(pl.multiple_of(step * piece, piece), piece), :]
        sig = 1.0 / (1.0 + jnp.exp(-pre))
        value = (pre * sig).astype(BF16).astype(F32)
        act[part, :] = value
        act_ref[part, :] = value
        grad = rows[part, :] * (sig * (1.0 + pre * (1.0 - sig)))
        grad_ref[part, :] = grad.astype(BF16)
        turned_ref[:, part] = grad.T.astype(BF16)
        return 0

    lax.fori_loop(0, block // piece, point, 0)

    @pl.when(turn == pl.num_programs(0) - 1)
    def _():
        copy_rows(levels * slots, 64, lambda r: list_ref[0, r], act, out)
        for level in range(levels):
            sends[level][...] = out[pl.ds(level * slots, slots), :].astype(BF16)


def weights_kernel(turned_ref, taken_ref, out_ref):
    wide = jnp.dot(turned_ref[...], taken_ref[...], preferred_element_type=F32)
    many = wide.shape[1] // LANES
    rows = out_ref.shape[0] // many
    for j in range(many):
        out_ref[pl.ds(j * rows, rows), :] = wide[:rows, j * LANES : (j + 1) * LANES].astype(BF16)


def unpack_kernel(full_ref, weights_ref, down_ref):
    kvol, chans, _ = weights_ref.shape
    noct, c2, _ = down_ref.shape
    centre = kvol // 2
    for k in range(kvol):
        spot = kvol - 1 if k == centre else k - int(k > centre)
        weights_ref[k] = full_ref[pl.ds(spot * chans, chans), :][:, :chans]
    first = kvol * chans
    rest = LANES - chans
    for o in range(noct - 1):
        down_ref[o] = full_ref[pl.ds(first + o * c2, c2), :][:, :chans]
    start = first + (noct - 1) * c2
    down_ref[noct - 1, pl.ds(0, c2 - rest), :] = full_ref[pl.ds(start, c2 - rest), :][:, :chans]
    lane = lax.broadcasted_iota(I32, (rest, LANES), 1)
    tail = jnp.zeros((rest, LANES), F32)
    for j in range(chans // rest):
        piece = pltpu.roll(full_ref[pl.ds(first + j * rest, rest), :], rest * (j + 1), 1)
        tail = jnp.where((lane >= j * rest) & (lane < (j + 1) * rest), piece, tail)
    down_ref[noct - 1, pl.ds(c2 - rest, rest), :] = tail[:, :chans]


def pool_kernel(levels, chans, keys_ref, self_ref, act_ref, grad_ref, weight_ref, *refs):
    received = refs[:levels]
    coarse_ref, down_ref, rows = refs[levels : levels + 3]
    pools = refs[levels + 3 :]
    slots = received[0].shape[0]
    noct, c2, _ = weight_ref.shape
    rest = LANES - chans
    ndev = grad_ref.shape[1]
    for level in range(levels):
        rows[pl.ds(level * slots, slots), :] = received[level][...].astype(F32)
    clear(pools)
    add_rows(act_ref.shape[0], 64, lambda r: self_ref[0, r], act_ref, pools)
    add_rows(levels * slots, 64, lambda r: keys_ref[0, r], rows, pools)
    coarse = jnp.zeros(coarse_ref.shape, F32)
    lane = lax.broadcasted_iota(I32, (rest, LANES), 1)
    for o in reversed(range(noct)):
        part = pl.ds(o * ndev, ndev)
        total = pools[0][part, :]
        for pool in pools[1:]:
            total = total + pool[part, :]
        pooled = total.astype(BF16)
        coarse = coarse + lax.dot_general(
            weight_ref[o], pooled, (((1,), (1,)), ((), ())), preferred_element_type=F32
        )
        down = jnp.dot(grad_ref[...], pooled, preferred_element_type=F32)
        if o == noct - 1:
            tail = down[c2 - rest :]
            down = down[: c2 - rest]
        if o == 0:
            parts = []
            for j in range(chans // rest):
                piece = pltpu.roll(tail, (chans - rest * j) % LANES, 1)
                parts.append(jnp.where(lane >= chans, piece, down[j * rest : (j + 1) * rest]))
            down = jnp.concatenate(parts + [down[chans:]], axis=0)
        down_ref[pl.ds(o * c2, down.shape[0]), :] = down.astype(BF16)
    coarse_ref[...] = coarse.astype(BF16)


def scatter_kernel(levels, halo, stages, index_ref, grad_ref, weight_ref, local_ref, *refs):
    backs = refs[:levels]
    buf0, buf1 = refs[levels : levels + 2]
    stores = refs[levels + 2 : levels + 2 + stages]
    tables = refs[levels + 2 + stages : -1]
    sems = refs[-1]
    bufs = (buf0, buf1)
    vdev = local_ref.shape[0]
    chunk = buf0.shape[0]
    lanes = len(tables)
    k = pl.program_id(0)
    last = pl.num_programs(0) - 1

    def ready(base, offset, buf):
        buf[...] = jnp.dot(grad_ref[pl.ds(base, chunk), :], weight_ref[offset], preferred_element_type=F32)

    @pl.when(k == 0)
    def _():
        clear(tables)
        ready(0, 0, buf0)

    def step(base, parity, store, entry):
        buf = bufs[parity]
        over = base + chunk == vdev
        ahead = pl.multiple_of(jnp.where(over, 0, base + chunk), chunk)
        ready(ahead, jnp.minimum(jnp.where(over, k + 1, k), last), bufs[1 - parity])
        for start in range(0, chunk, lanes):
            now = min(lanes, chunk - start)
            spots = [store[0, entry + start + j] for j in range(now)]
            sums = [tables[j][pl.ds(spots[j], 1), :] + buf[pl.ds(start + j, 1), :] for j in range(now)]
            for j in range(now):
                tables[j][pl.ds(spots[j], 1), :] = sums[j]

    walk(index_ref, stores, sems, vdev, chunk, last + 1, step)

    @pl.when(k == last)
    def _():
        def total(part):
            result = tables[0][part, :]
            for table in tables[1:]:
                result = result + table[part, :]
            return result

        def close(step, _):
            part = pl.ds(pl.multiple_of(step * chunk, chunk), chunk)
            centre = jnp.dot(grad_ref[part, :], weight_ref[last + 1], preferred_element_type=F32)
            local_ref[part, :] = total(part) + centre
            return 0

        lax.fori_loop(0, vdev // chunk, close, 0)
        for level in range(levels):
            backs[level][...] = total(pl.ds(vdev + level * halo, halo)).astype(BF16)


def finish_kernel(levels, rows_ref, local_ref, *refs):
    incoming = refs[:levels]
    out_ref, rows = refs[levels : levels + 2]
    tables = refs[levels + 2 :]
    halo = incoming[0].shape[0]
    chans, vdev = out_ref.shape
    for level in range(levels):
        rows[pl.ds(level * halo, halo), :] = incoming[level][...].astype(F32)
    clear(tables)
    add_rows(levels * halo, 64, lambda r: rows_ref[0, r], rows, tables)

    def close(step, _):
        part = pl.ds(pl.multiple_of(step * 2 * LANES, 2 * LANES), 2 * LANES)
        total = local_ref[part, :]
        for table in tables:
            total = total + table[part, :]
        out_ref[:, part] = total.T[:chans]
        return 0

    lax.fori_loop(0, vdev // (2 * LANES), close, 0)


def shape(dims, dtype):
    return jax.ShapeDtypeStruct(dims, dtype)


def params():
    return pltpu.CompilerParams(vmem_limit_bytes=56 << 20)


def shards(feats, kmap, send_rows, w_sub, owner, coarse_id, octant, w_down, grad_coarse):
    chans, vdev = feats.shape
    _, levels, halo = send_rows.shape
    kvol = kmap.shape[0]
    noct, c2, _ = w_down.shape
    coarse_dev = grad_coarse.shape[1]
    keys = noct * coarse_dev
    slots = vdev // 32
    bits_member = lax.axis_size("member").bit_length() - 1
    myself = lax.axis_index(("group", "member")).astype(I32).reshape(1)
    lane_pad = LANES - chans
    outgoing = send_rows.reshape(1, levels * halo)
    table_rows = vdev + levels * halo + SUB
    middle_k = kvol // 2
    index = jnp.concatenate([kmap[:middle_k], kmap[middle_k + 1 :]], axis=0).reshape(kvol - 1, 1, vdev)

    w_ordered = jnp.concatenate([w_sub[:middle_k], w_sub[middle_k + 1 :], w_sub[middle_k : middle_k + 1]], axis=0)
    w_backward = jnp.pad(w_ordered, ((0, 0), (0, lane_pad), (0, lane_pad)))
    w_forward = w_backward.transpose(0, 2, 1).reshape(kvol * LANES, LANES)
    down_pad = jnp.pad(w_down, ((0, 0), (0, 0), (0, lane_pad)))

    prepared = pl.pallas_call(
        functools.partial(prepare_kernel, levels, noct=noct, coarse_dev=coarse_dev, slots=slots),
        in_specs=[pl.BlockSpec(memory_space=SMEM), smem_full((1, levels * halo))]
        + [vmem_full((1, vdev))] * 3
        + [vmem_full((chans, vdev))],
        out_specs=[vmem_full((halo + 2 * SUB, LANES))] * levels
        + [vmem_full((vdev, LANES)), vmem_full((1, vdev)), vmem_full((1, levels * slots))],
        out_shape=[shape((halo + 2 * SUB, LANES), BF16)] * levels
        + [shape((vdev, LANES), F32), shape((1, vdev), I32), shape((1, levels * slots), I32)],
        scratch_shapes=[pltpu.VMEM((1, vdev), I32), pltpu.VMEM((levels * halo, LANES), F32)],
        compiler_params=params(),
        name="prepare",
    )(myself, outgoing, owner.reshape(1, vdev), coarse_id.reshape(1, vdev), octant.reshape(1, vdev), feats)
    messages = prepared[:levels]
    table, own_key, send_list = prepared[levels:]
    received = [from_partner(messages[level], level, bits_member) for level in range(levels)]

    wide, rows = pl.pallas_call(
        parents_kernel,
        in_specs=[smem_full((1, vdev)), vmem_full((coarse_dev, c2)), vmem_full((noct, c2, LANES))],
        out_specs=[vmem_full((keys + SUB, LANES)), vmem_full((vdev, LANES))],
        out_shape=[shape((keys + SUB, LANES), F32), shape((vdev, LANES), F32)],
        compiler_params=params(),
        name="parents",
    )(own_key, grad_coarse.T, down_pad)

    *received, index, w_forward, w_backward, wide, rows = lax.optimization_barrier(
        (*received, index, w_forward, w_backward, wide, rows)
    )
    digits = jnp.stack([got[halo : halo + 2] for got in received]).astype(F32)
    got_keys = (digits[:, 0] * DIGIT + digits[:, 1]).astype(I32).reshape(1, levels * slots)
    answers = pl.pallas_call(
        functools.partial(answer_kernel, levels),
        in_specs=[smem_full((1, levels * slots)), vmem_full((keys + SUB, LANES))],
        out_specs=[vmem_full((slots, LANES))] * levels,
        out_shape=[shape((slots, LANES), BF16)] * levels,
        scratch_shapes=[pltpu.VMEM((levels * slots, LANES), F32)],
        compiler_params=params(),
        name="answer",
    )(got_keys, wide)
    returned = [from_partner(answers[level], level, bits_member) for level in range(levels)]

    stages, width, chunk = 4, 1024, 512
    staging = [pltpu.SMEM((1, width), I32)] * stages
    gathered = pl.pallas_call(
        functools.partial(gather_kernel, levels, halo),
        grid=(kvol,),
        in_specs=[
            pl.BlockSpec(memory_space=pl.ANY),
            vmem_full((vdev, LANES)),
        ]
        + [vmem_full((halo + 2 * SUB, LANES))] * levels,
        out_specs=pl.BlockSpec((vdev, LANES), lambda k: (0, k)),
        out_shape=shape((vdev, kvol * LANES), BF16),
        scratch_shapes=[pltpu.VMEM((table_rows, LANES), F32)]
        + [pltpu.VMEM((chunk, LANES), F32)] * 2
        + staging
        + [pltpu.SemaphoreType.DMA((stages,))],
        compiler_params=params(),
        cost_estimate=pl.CostEstimate(flops=0, bytes_accessed=300_000_000, transcendentals=0),
        name="gather",
    )(index, table, *received)

    block = vdev // 4
    middle = pl.pallas_call(
        functools.partial(middle_kernel, levels),
        grid=(vdev // block,),
        in_specs=[
            smem_full((1, levels * slots)),
            pl.BlockSpec((block, kvol * LANES), lambda i: (i, 0)),
            vmem_full((kvol * LANES, LANES)),
            vmem_full((vdev, LANES)),
        ]
        + [vmem_full((slots, LANES))] * levels,
        out_specs=[vmem_full((vdev, LANES)), vmem_full((LANES, vdev)), vmem_full((vdev, LANES))]
        + [vmem_full((slots, LANES))] * levels,
        out_shape=[shape((vdev, LANES), BF16), shape((LANES, vdev), BF16), shape((vdev, LANES), F32)]
        + [shape((slots, LANES), BF16)] * levels,
        scratch_shapes=[
            pltpu.VMEM((vdev + SUB, LANES), F32),
            pltpu.VMEM((levels * slots, LANES), F32),
            pltpu.VMEM((vdev + SUB, LANES), F32),
            pltpu.VMEM((levels * slots, LANES), F32),
            pltpu.VMEM((block, LANES), F32),
        ],
        compiler_params=params(),
        cost_estimate=pl.CostEstimate(flops=0, bytes_accessed=40_000_000, transcendentals=0),
        name="middle",
    )(send_list, gathered, w_forward, rows, *returned)
    grad_pre, grad_turned, act = middle[:3]
    came = [from_partner(middle[3 + level], level, bits_member) for level in range(levels)]

    group = 3
    grad_w = pl.pallas_call(
        weights_kernel,
        grid=(kvol // group,),
        in_specs=[vmem_full((LANES, vdev)), pl.BlockSpec((vdev, group * LANES), lambda k: (0, k))],
        out_specs=pl.BlockSpec((group * chans, LANES), lambda k: (k, 0)),
        out_shape=shape((kvol * chans, LANES), BF16),
        compiler_params=params(),
        cost_estimate=pl.CostEstimate(flops=0, bytes_accessed=40_000_000, transcendentals=0),
        name="weights",
    )(grad_turned, gathered)

    coarse_out, grad_down = pl.pallas_call(
        functools.partial(pool_kernel, levels, chans),
        in_specs=[
            smem_full((1, levels * slots)),
            smem_full((1, vdev)),
            vmem_full((vdev, LANES)),
            vmem_full((c2, coarse_dev)),
            vmem_full((noct, c2, LANES)),
        ]
        + [vmem_full((slots, LANES))] * levels,
        out_specs=[vmem_full((c2, coarse_dev)), vmem_full((noct * c2 - lane_pad, LANES))],
        out_shape=[shape((c2, coarse_dev), BF16), shape((noct * c2 - lane_pad, LANES), BF16)],
        scratch_shapes=[pltpu.VMEM((levels * slots, LANES), F32)]
        + [pltpu.VMEM((keys + SUB, LANES), F32)] * 8,
        compiler_params=params(),
        name="pool",
    )(got_keys, own_key, act, grad_coarse, down_pad, *came)

    both = ("group", "member")
    devices = lax.axis_size(both)
    packed = jnp.concatenate([grad_w, grad_down], axis=0)
    share = packed.shape[0] // devices
    parts = lax.all_to_all(
        packed.reshape(devices, share, LANES), both, split_axis=0, concat_axis=0, tiled=True
    )
    summed = jnp.sum(parts.astype(F32), axis=0)
    summed, grad_pre = lax.optimization_barrier((summed, grad_pre))
    full = lax.all_gather(summed, both, axis=0, tiled=True)

    accumulators = 8
    scattered = pl.pallas_call(
        functools.partial(scatter_kernel, levels, halo, stages),
        grid=(kvol - 1,),
        in_specs=[
            pl.BlockSpec(memory_space=pl.ANY),
            vmem_full((vdev, LANES)),
            vmem_full((kvol, LANES, LANES)),
        ],
        out_specs=[vmem_full((vdev, LANES))] + [vmem_full((halo, LANES))] * levels,
        out_shape=[shape((vdev, LANES), F32)] + [shape((halo, LANES), BF16)] * levels,
        scratch_shapes=[pltpu.VMEM((chunk, LANES), F32)] * 2
        + staging
        + [pltpu.VMEM((table_rows, LANES), F32)] * accumulators
        + [pltpu.SemaphoreType.DMA((stages,))],
        compiler_params=params(),
        cost_estimate=pl.CostEstimate(flops=0, bytes_accessed=400_000_000, transcendentals=0),
        name="scatter",
    )(index, grad_pre, w_backward)
    incoming = [from_partner(scattered[1 + level], level, bits_member) for level in range(levels)]

    grad_w, grad_down = pl.pallas_call(
        unpack_kernel,
        in_specs=[vmem_full((devices * share, LANES))],
        out_specs=[vmem_full((kvol, chans, chans)), vmem_full((noct, c2, chans))],
        out_shape=[shape((kvol, chans, chans), F32), shape((noct, c2, chans), F32)],
        compiler_params=params(),
        name="unpack",
    )(full)
    *incoming, grad_w, grad_down = lax.optimization_barrier((*incoming, grad_w, grad_down))

    grad_feats = pl.pallas_call(
        functools.partial(finish_kernel, levels),
        in_specs=[smem_full((1, levels * halo)), vmem_full((vdev, LANES))] + [vmem_full((halo, LANES))] * levels,
        out_specs=vmem_full((chans, vdev)),
        out_shape=shape((chans, vdev), F32),
        scratch_shapes=[pltpu.VMEM((levels * halo, LANES), F32)] + [pltpu.VMEM((vdev, LANES), F32)] * 4,
        compiler_params=params(),
        name="finish",
    )(outgoing, scattered[0], *incoming)
    return coarse_out, grad_feats, grad_w, grad_down


def solution(mesh):
    both = ("group", "member")
    in_specs = (
        P(None, both),
        P(None, both),
        P(both, None, None),
        P(),
        P(both, None),
        P(both),
        P(both),
        P(),
        P(None, both),
    )
    out_specs = (P(None, both), P(None, both), P(), P())
    return jax.shard_map(shards, mesh=mesh, in_specs=in_specs, out_specs=out_specs, check_vma=False)
```

```python
import functools

import jax
import jax.numpy as jnp
from jax import lax
from jax.experimental import pallas as pl
from jax.experimental.pallas import tpu as pltpu
from jax.sharding import PartitionSpec as P

LANES = 128
SUB = 8
DIGIT = 64
SMEM = pltpu.SMEM
F32 = jnp.float32
BF16 = jnp.bfloat16
I32 = jnp.int32


def from_partner(value, level, bits_member):
    axis, stride = ("member", level) if level < bits_member else ("group", level - bits_member)
    mask = 2**stride
    pairs = [(source, source ^ mask) for source in range(lax.axis_size(axis))]
    return lax.ppermute(value, axis, pairs)


def vmem_full(shape):
    return pl.BlockSpec(shape, lambda *_: (0,) * len(shape))


def smem_full(shape):
    return pl.BlockSpec(shape, lambda *_: (0,) * len(shape), memory_space=SMEM)


def clear(tables):
    count = tables[0].shape[0]
    block = max(b for b in range(SUB, 257, SUB) if count % b == 0)

    def body(step, _):
        part = pl.ds(pl.multiple_of(step * block, block), block)
        for table in tables:
            table[part, :] = jnp.zeros((block, LANES), F32)
        return 0

    lax.fori_loop(0, count // block, body, 0)


def copy_rows(count, unroll, index, source, target):
    def body(step, _):
        base = pl.multiple_of(step * unroll, unroll)
        for j in range(unroll):
            target[pl.ds(base + j, 1), :] = source[pl.ds(index(base + j), 1), :]
        return 0

    lax.fori_loop(0, count // unroll, body, 0)


def add_rows(count, unroll, index, source, tables):
    lanes = len(tables)

    def body(step, _):
        base = pl.multiple_of(step * unroll, unroll)
        for start in range(0, unroll, lanes):
            spots = [index(base + start + j) for j in range(lanes)]
            sums = [
                tables[j][pl.ds(spots[j], 1), :] + source[pl.ds(base + start + j, 1), :]
                for j in range(lanes)
            ]
            for j in range(lanes):
                tables[j][pl.ds(spots[j], 1), :] = sums[j]
        return 0

    lax.fori_loop(0, count // unroll, body, 0)


def prepare_kernel(levels, me_ref, rows_ref, owner_ref, coarse_ref, octant_ref, feats_ref, *refs, noct, coarse_dev, slots):
    messages = refs[:levels]
    table_ref, self_ref, list_ref, pos_ref, buf = refs[levels:]
    chans, vdev = feats_ref.shape
    halo = rows_ref.shape[1] // levels
    noct_keys = noct * coarse_dev
    fill = jnp.zeros((LANES - chans, LANES), F32)
    for c in range(vdev // LANES):
        cols = pl.ds(c * LANES, LANES)
        block = jnp.concatenate([feats_ref[:, cols].astype(F32), fill], axis=0)
        table_ref[cols, :] = block.T
    copy_rows(levels * halo, 64, lambda r: rows_ref[0, r], table_ref, buf)

    differ = jnp.bitwise_xor(owner_ref[...], me_ref[0])
    level_id = lax.broadcasted_iota(I32, (SUB, LANES), 0)
    bit = jnp.where(level_id < levels, jnp.left_shift(jnp.ones_like(level_id), level_id), 0)
    chunks = vdev // LANES
    classes = []
    for c in range(chunks):
        part = jnp.broadcast_to(differ[:, c * LANES : (c + 1) * LANES], (SUB, LANES))
        classes.append(jnp.where((part == bit) & (level_id < levels), 1.0, 0.0).astype(F32))
    upper = lax.broadcasted_iota(I32, (LANES, LANES), 0) <= lax.broadcasted_iota(I32, (LANES, LANES), 1)
    prefix = jnp.dot(
        jnp.concatenate(classes, axis=0).astype(BF16),
        jnp.where(upper, 1.0, 0.0).astype(BF16),
        preferred_element_type=F32,
    )
    carry = jnp.zeros((SUB, 1), F32)
    start = (level_id * slots).astype(F32)
    digit_rows = []
    digit_id = lax.broadcasted_iota(I32, (SUB, LANES), 0)
    for c in range(chunks):
        cols = pl.ds(c * LANES, LANES)
        inclusive = prefix[c * SUB : (c + 1) * SUB]
        spot = classes[c] * (start + inclusive - 1.0 + carry)
        carry = carry + inclusive[:, LANES - 1 :]
        remote = jnp.sum(classes[c], axis=0, keepdims=True) > 0.5
        position = jnp.where(remote, jnp.sum(spot, axis=0, keepdims=True).astype(I32), levels * slots)
        keys = octant_ref[:, cols] * coarse_dev + coarse_ref[:, cols]
        pos_ref[:, cols] = position
        self_ref[:, cols] = jnp.where(remote, noct_keys, keys)
        voxel = lax.broadcasted_iota(I32, (SUB, LANES), 1) + c * LANES
        number = jnp.where(digit_id < 2, jnp.broadcast_to(keys, (SUB, LANES)), voxel)
        high = lax.shift_right_logical(number, 6) - DIGIT
        low = number & (DIGIT - 1)
        digits = jnp.where(digit_id < 4, jnp.where((digit_id & 1) == 0, high, low), 0)
        digit_rows.append(digits.astype(F32).astype(BF16))
    digits = jnp.concatenate(digit_rows, axis=1)
    slot_id = lax.broadcasted_iota(I32, (slots, LANES), 0)
    for level in range(levels):
        hot = []
        for c in range(chunks):
            position = jnp.broadcast_to(pos_ref[:, pl.ds(c * LANES, LANES)], (slots, LANES))
            hot.append(jnp.where(position == slot_id + level * slots, 1.0, 0.0).astype(BF16))
        found = lax.dot_general(
            digits, jnp.concatenate(hot, axis=1), (((1,), (1,)), ((), ())), preferred_element_type=F32
        )
        found = found + jnp.where((digit_id & 1) == 0, float(DIGIT), 0.0)
        list_ref[:, pl.ds(level * slots, slots)] = (found[2:3] * float(DIGIT) + found[3:4]).astype(I32)
        messages[level][pl.ds(0, halo), :] = buf[pl.ds(level * halo, halo), :].astype(BF16)
        messages[level][pl.ds(halo, 2 * SUB), :] = jnp.concatenate(
            [found, jnp.zeros((SUB, LANES), F32)], axis=0
        ).astype(BF16)


def parents_kernel(self_ref, coarse_ref, weight_ref, wide_ref, rows_ref):
    noct = weight_ref.shape[0]
    ndev = coarse_ref.shape[0]
    for o in range(noct):
        grad = jnp.dot(coarse_ref[...], weight_ref[o], preferred_element_type=F32)
        wide_ref[pl.ds(o * ndev, ndev), :] = grad.astype(BF16).astype(F32)
    wide_ref[pl.ds(noct * ndev, SUB), :] = jnp.zeros((SUB, LANES), F32)
    copy_rows(rows_ref.shape[0], 64, lambda r: self_ref[0, r], wide_ref, rows_ref)


def answer_kernel(levels, keys_ref, wide_ref, *refs):
    outs = refs[:levels]
    buf = refs[levels]
    slots = outs[0].shape[0]
    copy_rows(levels * slots, 64, lambda r: keys_ref[0, r], wide_ref, buf)
    for level in range(levels):
        outs[level][...] = buf[pl.ds(level * slots, slots), :].astype(BF16)


def index_copy(index_ref, piece, store, sem, width):
    pieces = index_ref.shape[2] // width
    row = lax.div(piece, pieces)
    start = pl.multiple_of(lax.rem(piece, pieces) * width, width)
    return pltpu.make_async_copy(index_ref.at[row, :, pl.ds(start, width)], store, sem)


def walk(index_ref, stores, sems, vdev, chunk, total, step_of):
    k = pl.program_id(0)
    width = stores[0].shape[1]
    many = len(stores)
    pieces = vdev // width

    @pl.when(k == 0)
    def _():
        for b in range(many):
            index_copy(index_ref, b, stores[b], sems.at[b], width).start()

    def body(turn, _):
        for b in range(many):
            piece = k * pieces + turn * many + b
            index_copy(index_ref, piece, stores[b], sems.at[b], width).wait()
            for sub in range(width // chunk):
                base = pl.multiple_of((turn * many + b) * width + sub * chunk, chunk)
                step_of(base, (b * (width // chunk) + sub) % 2, stores[b], sub * chunk)

            @pl.when(piece + many < total * pieces)
            def _():
                index_copy(index_ref, piece + many, stores[b], sems.at[b], width).start()

        return 0

    lax.fori_loop(0, pieces // many, body, 0)


def gather_kernel(levels, halo, index_ref, local_ref, *refs):
    received = refs[:levels]
    out_ref, table, buf0, buf1 = refs[levels : levels + 4]
    stores = refs[levels + 4 : -1]
    sems = refs[-1]
    bufs = (buf0, buf1)
    vdev = local_ref.shape[0]
    chunk = buf0.shape[0]

    @pl.when(pl.program_id(0) == 0)
    def _():
        table[pl.ds(0, vdev), :] = local_ref[...]
        for level in range(levels):
            table[pl.ds(vdev + level * halo, halo), :] = received[level][pl.ds(0, halo), :].astype(F32)
        table[pl.ds(vdev + levels * halo, SUB), :] = jnp.zeros((SUB, LANES), F32)
        buf1[...] = jnp.zeros_like(buf1)

    last = pl.num_programs(0) - 1

    def step(base, parity, store, entry):
        buf = bufs[parity]
        for j in range(chunk):
            buf[pl.ds(j, 1), :] = table[pl.ds(store[0, entry + j], 1), :]
        behind = pl.multiple_of(jnp.maximum(base - chunk, 0), chunk)
        out_ref[pl.ds(behind, chunk), :] = bufs[1 - parity][...].astype(BF16)

    @pl.when(pl.program_id(0) < last)
    def _():
        walk(index_ref, stores, sems, vdev, chunk, last, step)
        out_ref[pl.ds(vdev - chunk, chunk), :] = buf1[...].astype(BF16)

    @pl.when(pl.program_id(0) == last)
    def _():
        out_ref[...] = local_ref[...].astype(BF16)


def middle_kernel(levels, list_ref, taken_ref, weight_ref, rows_ref, *refs):
    returned = refs[:levels]
    grad_ref, turned_ref, act_ref = refs[levels : levels + 3]
    sends = refs[levels + 3 : 2 * levels + 3]
    rows, back, act, out, pre_buf = refs[2 * levels + 3 :]
    vdev = rows_ref.shape[0]
    slots = returned[0].shape[0]
    block = taken_ref.shape[0]
    piece = 2 * LANES
    turn = pl.program_id(0)

    @pl.when(turn == 0)
    def _():
        rows[pl.ds(0, vdev), :] = rows_ref[...]
        for level in range(levels):
            back[pl.ds(level * slots, slots), :] = returned[level][...].astype(F32)

        def patch(step, _):
            base = pl.multiple_of(step * 64, 64)
            for j in range(64):
                rows[pl.ds(list_ref[0, base + j], 1), :] = back[pl.ds(base + j, 1), :]
            return 0

        lax.fori_loop(0, levels * slots // 64, patch, 0)
        act[pl.ds(vdev, SUB), :] = jnp.zeros((SUB, LANES), F32)

    pre_buf[...] = jnp.dot(taken_ref[...], weight_ref[...], preferred_element_type=F32)

    def point(step, _):
        part = pl.ds(pl.multiple_of(turn * block + step * piece, piece), piece)
        pre = pre_buf[pl.ds(pl.multiple_of(step * piece, piece), piece), :]
        sig = 1.0 / (1.0 + jnp.exp(-pre))
        value = (pre * sig).astype(BF16).astype(F32)
        act[part, :] = value
        act_ref[part, :] = value
        grad = rows[part, :] * (sig * (1.0 + pre * (1.0 - sig)))
        grad_ref[part, :] = grad.astype(BF16)
        turned_ref[:, part] = grad.T.astype(BF16)
        return 0

    lax.fori_loop(0, block // piece, point, 0)

    @pl.when(turn == pl.num_programs(0) - 1)
    def _():
        copy_rows(levels * slots, 64, lambda r: list_ref[0, r], act, out)
        for level in range(levels):
            sends[level][...] = out[pl.ds(level * slots, slots), :].astype(BF16)


def weights_kernel(turned_ref, taken_ref, out_ref):
    wide = jnp.dot(turned_ref[...], taken_ref[...], preferred_element_type=F32)
    many = wide.shape[1] // LANES
    rows = out_ref.shape[0] // many
    for j in range(many):
        out_ref[pl.ds(j * rows, rows), :] = wide[:rows, j * LANES : (j + 1) * LANES].astype(BF16)


def unpack_kernel(full_ref, weights_ref, down_ref):
    kvol, chans, _ = weights_ref.shape
    noct, c2, _ = down_ref.shape
    for k in range(kvol):
        weights_ref[k] = full_ref[pl.ds(k * chans, chans), :][:, :chans]
    first = kvol * chans
    rest = LANES - chans
    for o in range(noct - 1):
        down_ref[o] = full_ref[pl.ds(first + o * c2, c2), :][:, :chans]
    start = first + (noct - 1) * c2
    down_ref[noct - 1, pl.ds(0, c2 - rest), :] = full_ref[pl.ds(start, c2 - rest), :][:, :chans]
    lane = lax.broadcasted_iota(I32, (rest, LANES), 1)
    tail = jnp.zeros((rest, LANES), F32)
    for j in range(chans // rest):
        piece = pltpu.roll(full_ref[pl.ds(first + j * rest, rest), :], rest * (j + 1), 1)
        tail = jnp.where((lane >= j * rest) & (lane < (j + 1) * rest), piece, tail)
    down_ref[noct - 1, pl.ds(c2 - rest, rest), :] = tail[:, :chans]


def pool_kernel(levels, chans, keys_ref, self_ref, act_ref, grad_ref, weight_ref, *refs):
    received = refs[:levels]
    coarse_ref, down_ref, rows = refs[levels : levels + 3]
    pools = refs[levels + 3 :]
    slots = received[0].shape[0]
    noct, c2, _ = weight_ref.shape
    rest = LANES - chans
    ndev = grad_ref.shape[1]
    for level in range(levels):
        rows[pl.ds(level * slots, slots), :] = received[level][...].astype(F32)
    clear(pools)
    add_rows(act_ref.shape[0], 64, lambda r: self_ref[0, r], act_ref, pools)
    add_rows(levels * slots, 64, lambda r: keys_ref[0, r], rows, pools)
    coarse = jnp.zeros(coarse_ref.shape, F32)
    lane = lax.broadcasted_iota(I32, (rest, LANES), 1)
    for o in reversed(range(noct)):
        part = pl.ds(o * ndev, ndev)
        total = pools[0][part, :]
        for pool in pools[1:]:
            total = total + pool[part, :]
        pooled = total.astype(BF16)
        coarse = coarse + lax.dot_general(
            weight_ref[o], pooled, (((1,), (1,)), ((), ())), preferred_element_type=F32
        )
        down = jnp.dot(grad_ref[...], pooled, preferred_element_type=F32)
        if o == noct - 1:
            tail = down[c2 - rest :]
            down = down[: c2 - rest]
        if o == 0:
            parts = []
            for j in range(chans // rest):
                piece = pltpu.roll(tail, (chans - rest * j) % LANES, 1)
                parts.append(jnp.where(lane >= chans, piece, down[j * rest : (j + 1) * rest]))
            down = jnp.concatenate(parts + [down[chans:]], axis=0)
        down_ref[pl.ds(o * c2, down.shape[0]), :] = down.astype(BF16)
    coarse_ref[...] = coarse.astype(BF16)


def scatter_kernel(levels, halo, stages, index_ref, grad_ref, weight_ref, local_ref, *refs):
    backs = refs[:levels]
    buf0, buf1 = refs[levels : levels + 2]
    stores = refs[levels + 2 : levels + 2 + stages]
    tables = refs[levels + 2 + stages : -1]
    sems = refs[-1]
    bufs = (buf0, buf1)
    vdev = local_ref.shape[0]
    chunk = buf0.shape[0]
    lanes = len(tables)
    k = pl.program_id(0)
    last = pl.num_programs(0) - 1
    middle_k = weight_ref.shape[0] // 2

    def ready(base, offset, buf):
        buf[...] = jnp.dot(grad_ref[pl.ds(base, chunk), :], weight_ref[offset + (offset >= middle_k).astype(I32)], preferred_element_type=F32)

    @pl.when(k == 0)
    def _():
        clear(tables)
        ready(0, jnp.int32(0), buf0)

    def step(base, parity, store, entry):
        buf = bufs[parity]
        over = base + chunk == vdev
        ahead = pl.multiple_of(jnp.where(over, 0, base + chunk), chunk)
        ready(ahead, jnp.minimum(jnp.where(over, k + 1, k), last), bufs[1 - parity])
        for start in range(0, chunk, lanes):
            now = min(lanes, chunk - start)
            spots = [store[0, entry + start + j] for j in range(now)]
            sums = [tables[j][pl.ds(spots[j], 1), :] + buf[pl.ds(start + j, 1), :] for j in range(now)]
            for j in range(now):
                tables[j][pl.ds(spots[j], 1), :] = sums[j]

    walk(index_ref, stores, sems, vdev, chunk, last + 1, step)

    @pl.when(k == last)
    def _():
        def total(part):
            result = tables[0][part, :]
            for table in tables[1:]:
                result = result + table[part, :]
            return result

        def close(step, _):
            part = pl.ds(pl.multiple_of(step * chunk, chunk), chunk)
            centre = jnp.dot(grad_ref[part, :], weight_ref[middle_k], preferred_element_type=F32)
            local_ref[part, :] = total(part) + centre
            return 0

        lax.fori_loop(0, vdev // chunk, close, 0)
        for level in range(levels):
            backs[level][...] = total(pl.ds(vdev + level * halo, halo)).astype(BF16)


def finish_kernel(levels, rows_ref, local_ref, *refs):
    incoming = refs[:levels]
    out_ref, rows = refs[levels : levels + 2]
    tables = refs[levels + 2 :]
    halo = incoming[0].shape[0]
    chans, vdev = out_ref.shape
    for level in range(levels):
        rows[pl.ds(level * halo, halo), :] = incoming[level][...].astype(F32)
    clear(tables)
    add_rows(levels * halo, 64, lambda r: rows_ref[0, r], rows, tables)

    def close(step, _):
        part = pl.ds(pl.multiple_of(step * 2 * LANES, 2 * LANES), 2 * LANES)
        total = local_ref[part, :]
        for table in tables:
            total = total + table[part, :]
        out_ref[:, part] = total.T[:chans]
        return 0

    lax.fori_loop(0, vdev // (2 * LANES), close, 0)


def shape(dims, dtype):
    return jax.ShapeDtypeStruct(dims, dtype)


def params():
    return pltpu.CompilerParams(vmem_limit_bytes=56 << 20)


def shards(feats, kmap, send_rows, w_sub, owner, coarse_id, octant, w_down, grad_coarse):
    chans, vdev = feats.shape
    _, levels, halo = send_rows.shape
    kvol = kmap.shape[0]
    noct, c2, _ = w_down.shape
    coarse_dev = grad_coarse.shape[1]
    keys = noct * coarse_dev
    slots = vdev // 32
    bits_member = lax.axis_size("member").bit_length() - 1
    myself = lax.axis_index(("group", "member")).astype(I32).reshape(1)
    lane_pad = LANES - chans
    outgoing = send_rows.reshape(1, levels * halo)
    table_rows = vdev + levels * halo + SUB
    middle_k = kvol // 2
    index = jnp.concatenate([kmap[:middle_k], kmap[middle_k + 1 :]], axis=0).reshape(kvol - 1, 1, vdev)

    w_backward = jnp.pad(w_sub, ((0, 0), (0, lane_pad), (0, lane_pad)))
    w_forward = w_backward.transpose(0, 2, 1).reshape(kvol * LANES, LANES)
    down_pad = jnp.pad(w_down, ((0, 0), (0, 0), (0, lane_pad)))

    prepared = pl.pallas_call(
        functools.partial(prepare_kernel, levels, noct=noct, coarse_dev=coarse_dev, slots=slots),
        in_specs=[pl.BlockSpec(memory_space=SMEM), smem_full((1, levels * halo))]
        + [vmem_full((1, vdev))] * 3
        + [vmem_full((chans, vdev))],
        out_specs=[vmem_full((halo + 2 * SUB, LANES))] * levels
        + [vmem_full((vdev, LANES)), vmem_full((1, vdev)), vmem_full((1, levels * slots))],
        out_shape=[shape((halo + 2 * SUB, LANES), BF16)] * levels
        + [shape((vdev, LANES), F32), shape((1, vdev), I32), shape((1, levels * slots), I32)],
        scratch_shapes=[pltpu.VMEM((1, vdev), I32), pltpu.VMEM((levels * halo, LANES), F32)],
        compiler_params=params(),
        name="prepare",
    )(myself, outgoing, owner.reshape(1, vdev), coarse_id.reshape(1, vdev), octant.reshape(1, vdev), feats)
    messages = prepared[:levels]
    table, own_key, send_list = prepared[levels:]
    received = [from_partner(messages[level], level, bits_member) for level in range(levels)]

    wide, rows = pl.pallas_call(
        parents_kernel,
        in_specs=[smem_full((1, vdev)), vmem_full((coarse_dev, c2)), vmem_full((noct, c2, LANES))],
        out_specs=[vmem_full((keys + SUB, LANES)), vmem_full((vdev, LANES))],
        out_shape=[shape((keys + SUB, LANES), F32), shape((vdev, LANES), F32)],
        compiler_params=params(),
        name="parents",
    )(own_key, grad_coarse.T, down_pad)

    *received, index, w_forward, w_backward, wide, rows = lax.optimization_barrier(
        (*received, index, w_forward, w_backward, wide, rows)
    )
    digits = jnp.stack([got[halo : halo + 2] for got in received]).astype(F32)
    got_keys = (digits[:, 0] * DIGIT + digits[:, 1]).astype(I32).reshape(1, levels * slots)
    answers = pl.pallas_call(
        functools.partial(answer_kernel, levels),
        in_specs=[smem_full((1, levels * slots)), vmem_full((keys + SUB, LANES))],
        out_specs=[vmem_full((slots, LANES))] * levels,
        out_shape=[shape((slots, LANES), BF16)] * levels,
        scratch_shapes=[pltpu.VMEM((levels * slots, LANES), F32)],
        compiler_params=params(),
        name="answer",
    )(got_keys, wide)
    returned = [from_partner(answers[level], level, bits_member) for level in range(levels)]

    stages, width, chunk = 4, 1024, 512
    staging = [pltpu.SMEM((1, width), I32)] * stages
    gathered = pl.pallas_call(
        functools.partial(gather_kernel, levels, halo),
        grid=(kvol,),
        in_specs=[
            pl.BlockSpec(memory_space=pl.ANY),
            vmem_full((vdev, LANES)),
        ]
        + [vmem_full((halo + 2 * SUB, LANES))] * levels,
        out_specs=pl.BlockSpec(
            (vdev, LANES), lambda k: (0, jnp.where(k == kvol - 1, middle_k, k + (k >= middle_k).astype(I32)))
        ),
        out_shape=shape((vdev, kvol * LANES), BF16),
        scratch_shapes=[pltpu.VMEM((table_rows, LANES), F32)]
        + [pltpu.VMEM((chunk, LANES), F32)] * 2
        + staging
        + [pltpu.SemaphoreType.DMA((stages,))],
        compiler_params=params(),
        cost_estimate=pl.CostEstimate(flops=0, bytes_accessed=300_000_000, transcendentals=0),
        name="gather",
    )(index, table, *received)

    block = vdev // 4
    middle = pl.pallas_call(
        functools.partial(middle_kernel, levels),
        grid=(vdev // block,),
        in_specs=[
            smem_full((1, levels * slots)),
            pl.BlockSpec((block, kvol * LANES), lambda i: (i, 0)),
            vmem_full((kvol * LANES, LANES)),
            vmem_full((vdev, LANES)),
        ]
        + [vmem_full((slots, LANES))] * levels,
        out_specs=[vmem_full((vdev, LANES)), vmem_full((LANES, vdev)), vmem_full((vdev, LANES))]
        + [vmem_full((slots, LANES))] * levels,
        out_shape=[shape((vdev, LANES), BF16), shape((LANES, vdev), BF16), shape((vdev, LANES), F32)]
        + [shape((slots, LANES), BF16)] * levels,
        scratch_shapes=[
            pltpu.VMEM((vdev + SUB, LANES), F32),
            pltpu.VMEM((levels * slots, LANES), F32),
            pltpu.VMEM((vdev + SUB, LANES), F32),
            pltpu.VMEM((levels * slots, LANES), F32),
            pltpu.VMEM((block, LANES), F32),
        ],
        compiler_params=params(),
        cost_estimate=pl.CostEstimate(flops=0, bytes_accessed=40_000_000, transcendentals=0),
        name="middle",
    )(send_list, gathered, w_forward, rows, *returned)
    grad_pre, grad_turned, act = middle[:3]
    came = [from_partner(middle[3 + level], level, bits_member) for level in range(levels)]

    group = 3
    grad_w = pl.pallas_call(
        weights_kernel,
        grid=(kvol // group,),
        in_specs=[vmem_full((LANES, vdev)), pl.BlockSpec((vdev, group * LANES), lambda k: (0, k))],
        out_specs=pl.BlockSpec((group * chans, LANES), lambda k: (k, 0)),
        out_shape=shape((kvol * chans, LANES), BF16),
        compiler_params=params(),
        cost_estimate=pl.CostEstimate(flops=0, bytes_accessed=40_000_000, transcendentals=0),
        name="weights",
    )(grad_turned, gathered)

    coarse_out, grad_down = pl.pallas_call(
        functools.partial(pool_kernel, levels, chans),
        in_specs=[
            smem_full((1, levels * slots)),
            smem_full((1, vdev)),
            vmem_full((vdev, LANES)),
            vmem_full((c2, coarse_dev)),
            vmem_full((noct, c2, LANES)),
        ]
        + [vmem_full((slots, LANES))] * levels,
        out_specs=[vmem_full((c2, coarse_dev)), vmem_full((noct * c2 - lane_pad, LANES))],
        out_shape=[shape((c2, coarse_dev), BF16), shape((noct * c2 - lane_pad, LANES), BF16)],
        scratch_shapes=[pltpu.VMEM((levels * slots, LANES), F32)]
        + [pltpu.VMEM((keys + SUB, LANES), F32)] * 8,
        compiler_params=params(),
        name="pool",
    )(got_keys, own_key, act, grad_coarse, down_pad, *came)

    both = ("group", "member")
    devices = lax.axis_size(both)
    packed = jnp.concatenate([grad_w, grad_down], axis=0)
    share = packed.shape[0] // devices
    parts = lax.all_to_all(
        packed.reshape(devices, share, LANES), both, split_axis=0, concat_axis=0, tiled=True
    )
    summed = jnp.sum(parts.astype(F32), axis=0)
    summed, grad_pre = lax.optimization_barrier((summed, grad_pre))
    full = lax.all_gather(summed, both, axis=0, tiled=True)

    accumulators = 8
    scattered = pl.pallas_call(
        functools.partial(scatter_kernel, levels, halo, stages),
        grid=(kvol - 1,),
        in_specs=[
            pl.BlockSpec(memory_space=pl.ANY),
            vmem_full((vdev, LANES)),
            vmem_full((kvol, LANES, LANES)),
        ],
        out_specs=[vmem_full((vdev, LANES))] + [vmem_full((halo, LANES))] * levels,
        out_shape=[shape((vdev, LANES), F32)] + [shape((halo, LANES), BF16)] * levels,
        scratch_shapes=[pltpu.VMEM((chunk, LANES), F32)] * 2
        + staging
        + [pltpu.VMEM((table_rows, LANES), F32)] * accumulators
        + [pltpu.SemaphoreType.DMA((stages,))],
        compiler_params=params(),
        cost_estimate=pl.CostEstimate(flops=0, bytes_accessed=400_000_000, transcendentals=0),
        name="scatter",
    )(index, grad_pre, w_backward)
    incoming = [from_partner(scattered[1 + level], level, bits_member) for level in range(levels)]

    grad_w, grad_down = pl.pallas_call(
        unpack_kernel,
        in_specs=[vmem_full((devices * share, LANES))],
        out_specs=[vmem_full((kvol, chans, chans)), vmem_full((noct, c2, chans))],
        out_shape=[shape((kvol, chans, chans), F32), shape((noct, c2, chans), F32)],
        compiler_params=params(),
        name="unpack",
    )(full)
    *incoming, grad_w, grad_down = lax.optimization_barrier((*incoming, grad_w, grad_down))

    grad_feats = pl.pallas_call(
        functools.partial(finish_kernel, levels),
        in_specs=[smem_full((1, levels * halo)), vmem_full((vdev, LANES))] + [vmem_full((halo, LANES))] * levels,
        out_specs=vmem_full((chans, vdev)),
        out_shape=shape((chans, vdev), F32),
        scratch_shapes=[pltpu.VMEM((levels * halo, LANES), F32)] + [pltpu.VMEM((vdev, LANES), F32)] * 4,
        compiler_params=params(),
        name="finish",
    )(outgoing, scattered[0], *incoming)
    return coarse_out, grad_feats, grad_w, grad_down


def solution(mesh):
    both = ("group", "member")
    in_specs = (
        P(None, both),
        P(None, both),
        P(both, None, None),
        P(),
        P(both, None),
        P(both),
        P(both),
        P(),
        P(None, both),
    )
    out_specs = (P(None, both), P(None, both), P(), P())
    return jax.shard_map(shards, mesh=mesh, in_specs=in_specs, out_specs=out_specs, check_vma=False)
```
